128 devices in a mesh: group: 16 (over z, y), inner: 8 (over x, core).
Axes of the slice: x: 4, y: 4, z: 4, core: 2. Of those that a mesh axis runs over, the one named last changes fastest.
Arguments:
- tokens: bfloat16 [16384, 7168], P(('group', 'inner')), may hold values from -6 to 6
- target: int32 [16384], P(('group', 'inner')), may hold values from 0 to 16, as said below
- gate_scale: float32 [16384], P(('group', 'inner')), may hold values from 0.25 to 2.5
- gate_weight: bfloat16 [16, 7168, 2048], P('group', None, 'inner'), may hold values from -0.0625 to 0.0625
- up_weight: bfloat16 [16, 7168, 2048], P('group', None, 'inner'), may hold values from -0.0625 to 0.0625
- down_weight: bfloat16 [16, 2048, 7168], P('group', 'inner'), may hold values from -0.125 to 0.125
Outputs:
- routed_out: bfloat16 [16384, 7168], P(('group', 'inner'))
The draws below stay inside these ranges and needn't reach their ends.
Inputs may be any that keep to these rules, and one draw needn't show every extreme that they name: 16 means that the token uses no expert of this round. Among the 128 tokens of one device at most 10 target any one group, and in every device some group is targeted by exactly 10 of them.
All inputs are finite; a program needn't handle non-finite values.
Results may differ from the reference program's by a relative error of at most 0.0095.
Values may be sent and summed in bfloat16 or wider, within the bound.
A program may use at most 192 MiB of HBM per device.

```python
import math
import jax
import jax.numpy as jnp
from jax import lax

D = 7168
FF = 2048
TOK_DEV = 128
EXPERTS = 16
CAP = 10
TOKENS = 16384
N_GROUP = 16
N_INNER = 8


def draw_target(key, part):
    blocks = N_GROUP * N_INNER
    key_hot, key_raw, key_mix = jax.random.split(jax.random.fold_in(key, 11), 3)
    hot_group = jax.random.randint(key_hot, (blocks, 1), 0, N_GROUP)
    raw_pick = jax.random.randint(key_raw, (blocks, TOK_DEV), 0, 2 * N_GROUP)
    position = jnp.arange(TOK_DEV, dtype=jnp.int32)[None, :]
    wanted = jnp.where(position < CAP, hot_group, raw_pick)
    wanted = jnp.where(wanted >= N_GROUP, N_GROUP, wanted)
    onehot = (wanted[:, :, None] == jnp.arange(N_GROUP, dtype=jnp.int32)[None, None, :]).astype(jnp.int32)
    before = jnp.sum((jnp.cumsum(onehot, axis=1) - onehot) * onehot, axis=2)
    wanted = jnp.where(before >= CAP, N_GROUP, wanted)
    scores = jax.random.randint(key_mix, (blocks, TOK_DEV), 0, 1 << 20) * TOK_DEV + position
    ordering = jnp.argsort(scores, axis=1, stable=True)
    return jnp.take_along_axis(wanted, ordering, axis=1).reshape(blocks * TOK_DEV).astype(jnp.int32)


def levels(rng, dims, shards, smallest, high):
    level = 1.0
    for dim, blocks in shards:
        steps = jax.random.uniform(jax.random.fold_in(jax.random.fold_in(rng, 6), dim), (blocks,), jnp.float32, smallest / len(shards), high / len(shards))
        level = level * jnp.repeat(jnp.exp(steps), dims[dim] // blocks).reshape((-1,) + (1,) * (len(dims) - 1 - dim))
    return level


def normal_values(stream_key, dims, width, limit, shards=(), kind=jnp.bfloat16):
    array = jax.random.normal(stream_key, dims, jnp.float32) * width
    if len(shards) > 0:
        array = levels(stream_key, dims, shards, -0.22, 0.18) * array
    return jnp.clip(array, min=-limit, max=limit).astype(kind)


def setup_inputs(seed: int = 0) -> dict:
    streams_of = jax.random.split(jax.random.key(seed), 7)
    return {
        "tokens": normal_values(streams_of[0], (TOKENS, D), 1.0, 6.0, ((0, 128),)),
        "target": draw_target(jax.random.fold_in(streams_of[6], 71), 0),
        "gate_scale": jnp.clip(jnp.exp(math.log(2.5) - 2.3025851 * jax.random.uniform(streams_of[2], (TOKENS,), jnp.float32) ** levels(streams_of[2], (TOKENS,), ((0, 128),), -0.2, 0.2)), 0.25, 2.5),
        "gate_weight": normal_values(streams_of[3], (EXPERTS, D, FF), D ** -0.5, 0.0625, ((0, 16), (2, 8))),
        "up_weight": normal_values(streams_of[4], (EXPERTS, D, FF), D ** -0.5, 0.0625, ((0, 16), (2, 8))),
        "down_weight": normal_values(streams_of[5], (EXPERTS, FF, D), FF ** -0.5, 0.125, ((0, 16), (1, 8))),
    }


def reference(tokens, target, gate_scale, gate_weight, up_weight, down_weight):
    slot_count = N_GROUP * N_INNER * CAP
    slice_width = FF // N_INNER

    def per_expert(inputs):
        expert_id, gate_mat, up_mat, down_mat = inputs
        is_hit = target == expert_id
        hit_count = jnp.sum(is_hit.astype(jnp.int32))
        row_index = jnp.nonzero(is_hit, size=slot_count, fill_value=0)[0].astype(jnp.int32)
        is_valid = jnp.arange(slot_count, dtype=jnp.int32) < hit_count
        picked = jnp.where(is_valid[:, None], tokens[row_index], jnp.zeros((), tokens.dtype))
        gate_pre = jnp.dot(picked, gate_mat, preferred_element_type=jnp.float32)
        up_pre = jnp.dot(picked, up_mat, preferred_element_type=jnp.float32)
        hidden = (jax.nn.silu(gate_pre) * up_pre).astype(jnp.bfloat16)
        hidden = hidden.reshape(slot_count, N_INNER, slice_width).astype(jnp.float32)
        down_parts = down_mat.reshape(N_INNER, slice_width, D).astype(jnp.float32)
        partials = jnp.einsum("mjk,jkd->mjd", hidden, down_parts).astype(jnp.bfloat16)
        partials = lax.optimization_barrier(partials)
        expert_out = jnp.sum(partials.astype(jnp.float32), axis=1).astype(jnp.bfloat16)
        expert_out = jnp.where(is_valid[:, None], expert_out, jnp.zeros((), expert_out.dtype))
        return row_index, expert_out

    row_index, outputs = lax.map(per_expert, (jnp.arange(N_GROUP, dtype=jnp.int32), gate_weight, up_weight, down_weight))
    scattered = jnp.zeros((TOKENS, D), jnp.float32).at[row_index.reshape(-1)].add(outputs.reshape(-1, D).astype(jnp.float32))
    return (gate_scale[:, None] * scattered).astype(jnp.bfloat16)
```

```python
import jax
import jax.numpy as jnp
from jax import lax
from jax.sharding import PartitionSpec as P


def expert_part(rows_in, gate_mat, up_mat, down_mat):
    gate_pre = jnp.dot(rows_in, gate_mat, preferred_element_type=jnp.float32)
    up_pre = jnp.dot(rows_in, up_mat, preferred_element_type=jnp.float32)
    hidden = (jax.nn.silu(gate_pre) * up_pre).astype(jnp.bfloat16)
    return jnp.dot(hidden, down_mat, preferred_element_type=jnp.float32)


def body(tokens, target, gate_scale, gate_weight, up_weight, down_weight):
    groups = lax.axis_size("group")
    inner_size = lax.axis_size("inner")
    tok_count = tokens.shape[0]
    model_width = tokens.shape[1]
    capacity = tok_count * 5 // (4 * groups)
    slot_count = groups * capacity
    onehot = (target[:, None] == jnp.arange(groups, dtype=jnp.int32)[None, :]).astype(jnp.int32)
    rank_in = jnp.sum((jnp.cumsum(onehot, axis=0) - onehot) * onehot, axis=1)
    slot_of = jnp.where(target < groups, target * capacity + rank_in, slot_count)
    dispatch = (slot_of[None, :] == jnp.arange(slot_count, dtype=jnp.int32)[:, None]).astype(
        jnp.bfloat16
    )
    outbound = jnp.dot(dispatch, tokens, preferred_element_type=jnp.float32).astype(jnp.bfloat16)
    outbound = outbound.reshape(groups, capacity, model_width)
    received = lax.all_to_all(outbound, "group", 0, 0, tiled=True)
    gathered = lax.all_gather(received, "inner", axis=0, tiled=False)
    partial_value = expert_part(
        gathered.reshape(-1, model_width), gate_weight[0], up_weight[0], down_weight[0]
    )
    partial_value = partial_value.astype(jnp.bfloat16).reshape(
        inner_size, groups, capacity, model_width
    )
    pieces = lax.all_to_all(partial_value, "inner", 0, 0, tiled=True)
    summed = jnp.sum(pieces.astype(jnp.float32), axis=0).astype(jnp.bfloat16)
    back_rows = lax.all_to_all(summed, "group", 0, 0, tiled=True).reshape(slot_count, model_width)
    expert_out = lax.dot_general(
        dispatch, back_rows, (((0,), (0,)), ((), ())), preferred_element_type=jnp.float32
    )
    return (gate_scale[:, None] * expert_out).astype(jnp.bfloat16)


def solution(mesh):
    in_specs = (
        P(("group", "inner"), None),
        P(("group", "inner")),
        P(("group", "inner")),
        P("group", None, "inner"),
        P("group", None, "inner"),
        P("group", "inner", None),
    )
    out_specs = P(("group", "inner"), None)
    return jax.shard_map(body, mesh=mesh, in_specs=in_specs, out_specs=out_specs, check_vma=False)
```

```python
import jax
import jax.numpy as jnp
from jax import lax
from jax.sharding import PartitionSpec as P


def expert_part(rows_in, gate_mat, up_mat, down_mat):
    gate_pre = jnp.einsum("abcd,df->abcf", rows_in, gate_mat, preferred_element_type=jnp.float32)
    up_pre = jnp.einsum("abcd,df->abcf", rows_in, up_mat, preferred_element_type=jnp.float32)
    hidden = (jax.nn.silu(gate_pre) * up_pre).astype(jnp.bfloat16)
    return jnp.einsum("abcf,fd->abcd", hidden, down_mat, preferred_element_type=jnp.float32)


def body(tokens, target, gate_scale, gate_weight, up_weight, down_weight):
    groups = lax.axis_size("group")
    inner_size = lax.axis_size("inner")
    tok_count = tokens.shape[0]
    model_width = tokens.shape[1]
    capacity = tok_count * 5 // (4 * groups)
    slot_count = groups * capacity
    onehot = (target[:, None] == jnp.arange(groups, dtype=jnp.int32)[None, :]).astype(jnp.int32)
    rank_in = jnp.sum((jnp.cumsum(onehot, axis=0) - onehot) * onehot, axis=1)
    slot_of = jnp.where(target < groups, target * capacity + rank_in, slot_count)
    dispatch = (slot_of[None, :] == jnp.arange(slot_count, dtype=jnp.int32)[:, None]).astype(
        jnp.bfloat16
    )
    outbound = jnp.dot(dispatch, tokens, preferred_element_type=jnp.float32).astype(jnp.bfloat16)
    outbound = outbound.reshape(groups, capacity, model_width)
    received = lax.all_to_all(outbound, "group", 0, 0, tiled=True)
    gathered = lax.all_gather(received, "inner", axis=0, tiled=False)
    partial_value = expert_part(gathered, gate_weight[0], up_weight[0], down_weight[0])
    partial_value = partial_value.astype(jnp.bfloat16)
    summed = lax.psum_scatter(partial_value, "inner", scatter_dimension=0, tiled=False)
    back_rows = lax.all_to_all(summed, "group", 0, 0, tiled=True)
    expert_out = jnp.einsum(
        "gct,gcd->td",
        dispatch.reshape(groups, capacity, tok_count),
        back_rows,
        preferred_element_type=jnp.float32,
    )
    return (gate_scale[:, None] * expert_out).astype(jnp.bfloat16)


def solution(mesh):
    in_specs = (
        P(("group", "inner"), None),
        P(("group", "inner")),
        P(("group", "inner")),
        P("group", None, "inner"),
        P("group", None, "inner"),
        P("group", "inner", None),
    )
    out_specs = P(("group", "inner"), None)
    return jax.shard_map(body, mesh=mesh, in_specs=in_specs, out_specs=out_specs, check_vma=False)
```

```python
import functools

import jax
import jax.numpy as jnp
from jax import lax
from jax.experimental import pallas as pl
from jax.experimental.pallas import tpu as pltpu
from jax.sharding import PartitionSpec as P

MESH = pl.DeviceIdType.MESH


def exchange_kernel(groups, x_ref, y_ref, local_sem, send_sem, recv_sem):
    me = lax.axis_index("group")
    inner = lax.axis_index("inner")
    barrier = pltpu.get_barrier_semaphore()
    for k in range(1, groups):
        peer = lax.rem(me + k, groups)
        pl.semaphore_signal(barrier, inc=1, device_id=(peer, inner), device_id_type=MESH)
    pl.semaphore_wait(barrier, groups - 1)
    local = pltpu.make_async_copy(x_ref.at[me], y_ref.at[me], local_sem)
    local.start()
    sends = []
    for k in range(1, groups):
        peer = lax.rem(me + k, groups)
        copy = pltpu.make_async_remote_copy(
            src_ref=x_ref.at[peer],
            dst_ref=y_ref.at[me],
            send_sem=send_sem.at[peer],
            recv_sem=recv_sem.at[me],
            device_id=(peer, inner),
            device_id_type=MESH,
        )
        copy.start()
        sends.append(copy)
    for k in range(1, groups):
        source = lax.rem(me + groups - k, groups)
        sends[k - 1].wait_send()
        pltpu.make_async_remote_copy(
            src_ref=x_ref.at[source],
            dst_ref=y_ref.at[source],
            send_sem=send_sem.at[source],
            recv_sem=recv_sem.at[source],
            device_id=(source, inner),
            device_id_type=MESH,
        ).wait_recv()
    local.wait()


def group_exchange(x, collective_id):
    groups = x.shape[0]
    return pl.pallas_call(
        functools.partial(exchange_kernel, groups),
        out_shape=jax.ShapeDtypeStruct(x.shape, x.dtype),
        in_specs=[pl.BlockSpec(memory_space=pl.ANY)],
        out_specs=pl.BlockSpec(memory_space=pl.ANY),
        scratch_shapes=[
            pltpu.SemaphoreType.DMA,
            pltpu.SemaphoreType.DMA((groups,)),
            pltpu.SemaphoreType.DMA((groups,)),
        ],
        compiler_params=pltpu.CompilerParams(collective_id=collective_id, has_side_effects=True),
    )(x)


def expert_part(rows_in, gate_mat, up_mat, down_mat):
    gate_pre = jnp.dot(rows_in, gate_mat, preferred_element_type=jnp.float32)
    up_pre = jnp.dot(rows_in, up_mat, preferred_element_type=jnp.float32)
    hidden = (jax.nn.silu(gate_pre) * up_pre).astype(jnp.bfloat16)
    return jnp.dot(hidden, down_mat, preferred_element_type=jnp.float32)


def body(tokens, target, gate_scale, gate_weight, up_weight, down_weight):
    groups = lax.axis_size("group")
    inner_size = lax.axis_size("inner")
    tok_count = tokens.shape[0]
    model_width = tokens.shape[1]
    capacity = tok_count * 5 // (4 * groups)
    slot_count = groups * capacity
    onehot = (target[:, None] == jnp.arange(groups, dtype=jnp.int32)[None, :]).astype(jnp.int32)
    rank_in = jnp.sum((jnp.cumsum(onehot, axis=0) - onehot) * onehot, axis=1)
    slot_of = jnp.where(target < groups, target * capacity + rank_in, slot_count)
    dispatch = (slot_of[None, :] == jnp.arange(slot_count, dtype=jnp.int32)[:, None]).astype(
        jnp.bfloat16
    )
    outbound = jnp.dot(dispatch, tokens, preferred_element_type=jnp.float32).astype(jnp.bfloat16)
    outbound = outbound.reshape(groups, capacity, model_width)
    received = group_exchange(outbound, 0)
    gathered = lax.all_gather(received.reshape(slot_count, model_width), "inner", axis=0, tiled=True)
    partial_value = expert_part(gathered, gate_weight[0], up_weight[0], down_weight[0])
    partial_value = partial_value.astype(jnp.bfloat16)
    summed = lax.psum_scatter(partial_value, "inner", scatter_dimension=0, tiled=True)
    back_rows = group_exchange(summed.reshape(groups, capacity, model_width), 1)
    expert_out = jnp.einsum(
        "gct,gcd->td",
        dispatch.reshape(groups, capacity, tok_count),
        back_rows,
        preferred_element_type=jnp.float32,
    )
    return (gate_scale[:, None] * expert_out).astype(jnp.bfloat16)


def solution(mesh):
    in_specs = (
        P(("group", "inner"), None),
        P(("group", "inner")),
        P(("group", "inner")),
        P("group", None, "inner"),
        P("group", None, "inner"),
        P("group", "inner", None),
    )
    out_specs = P(("group", "inner"), None)
    return jax.shard_map(body, mesh=mesh, in_specs=in_specs, out_specs=out_specs, check_vma=False)
```

```python
import functools

import jax
import jax.numpy as jnp
from jax import lax
from jax.experimental import pallas as pl
from jax.experimental.pallas import tpu as pltpu
from jax.sharding import PartitionSpec as P

MESH = pl.DeviceIdType.MESH


def chunk_orders(groups):
    pairs = [(k, groups - k) for k in range(1, (groups + 1) // 2)]
    first = [0] + ([groups // 2] if groups % 2 == 0 and groups > 1 else [])
    second = []
    for index, pair in enumerate(pairs):
        (first if index < len(pairs) // 2 else second).extend(pair)
    return [first, second] if second else [first]


def exchange_kernel(groups, offsets, src_base, sign, x_ref, y_ref, local_sem, send_sem, recv_sem):
    me = lax.axis_index("group")
    inner = lax.axis_index("inner")
    peers = sorted({k % groups for k in offsets} - {0})
    barrier = pltpu.get_barrier_semaphore()
    for k in peers:
        pl.semaphore_signal(
            barrier, inc=1, device_id=(lax.rem(me + k, groups), inner), device_id_type=MESH
        )
    if peers:
        pl.semaphore_wait(barrier, len(peers))
    local = None
    sends = []
    for i, k in enumerate(offsets):
        if k == 0:
            local = pltpu.make_async_copy(x_ref.at[src_base + i], y_ref.at[i], local_sem)
            local.start()
            continue
        dest = lax.rem(me + sign * k + groups, groups)
        copy = pltpu.make_async_remote_copy(
            src_ref=x_ref.at[src_base + i],
            dst_ref=y_ref.at[i],
            send_sem=send_sem.at[i],
            recv_sem=recv_sem.at[i],
            device_id=(dest, inner),
            device_id_type=MESH,
        )
        copy.start()
        sends.append(copy)
    for copy in sends:
        copy.wait_send()
    for i, k in enumerate(offsets):
        if k == 0:
            continue
        source = lax.rem(me - sign * k + groups, groups)
        pltpu.make_async_remote_copy(
            src_ref=x_ref.at[src_base + i],
            dst_ref=y_ref.at[i],
            send_sem=send_sem.at[i],
            recv_sem=recv_sem.at[i],
            device_id=(source, inner),
            device_id_type=MESH,
        ).wait_recv()
    if local is not None:
        local.wait()


def group_exchange(x, offsets, src_base, sign, collective_id):
    groups = lax.axis_size("group")
    count = len(offsets)
    return pl.pallas_call(
        functools.partial(exchange_kernel, groups, tuple(offsets), src_base, sign),
        out_shape=jax.ShapeDtypeStruct((count,) + x.shape[1:], x.dtype),
        in_specs=[pl.BlockSpec(memory_space=pl.ANY)],
        out_specs=pl.BlockSpec(memory_space=pl.ANY),
        scratch_shapes=[
            pltpu.SemaphoreType.DMA,
            pltpu.SemaphoreType.DMA((count,)),
            pltpu.SemaphoreType.DMA((count,)),
        ],
        compiler_params=pltpu.CompilerParams(collective_id=collective_id, has_side_effects=True),
    )(x)


def expert_part(rows_in, gate_mat, up_mat, down_mat):
    gate_pre = jnp.dot(rows_in, gate_mat, preferred_element_type=jnp.float32)
    up_pre = jnp.dot(rows_in, up_mat, preferred_element_type=jnp.float32)
    hidden = (jax.nn.silu(gate_pre) * up_pre).astype(jnp.bfloat16)
    return jnp.dot(hidden, down_mat, preferred_element_type=jnp.float32)


def body(tokens, target, gate_scale, gate_weight, up_weight, down_weight):
    groups = lax.axis_size("group")
    tok_count = tokens.shape[0]
    model_width = tokens.shape[1]
    capacity = tok_count * 5 // (4 * groups)
    slot_count = groups * capacity
    chunks = chunk_orders(groups)
    order = [k for chunk in chunks for k in chunk]
    position_of = [0] * groups
    for position, k in enumerate(order):
        position_of[k] = position
    me = lax.axis_index("group")
    onehot = (target[:, None] == jnp.arange(groups, dtype=jnp.int32)[None, :]).astype(jnp.int32)
    rank_in = jnp.sum((jnp.cumsum(onehot, axis=0) - onehot) * onehot, axis=1)
    relative = lax.rem(target - me + groups, groups)
    position = jnp.asarray(position_of, dtype=jnp.int32)[relative]
    slot_of = jnp.where(target < groups, position * capacity + rank_in, slot_count)
    dispatch = (slot_of[None, :] == jnp.arange(slot_count, dtype=jnp.int32)[:, None]).astype(
        jnp.bfloat16
    )
    outbound = jnp.dot(dispatch, tokens, preferred_element_type=jnp.float32).astype(jnp.bfloat16)
    outbound = outbound.reshape(groups, capacity, model_width)
    returned = []
    base = 0
    for index, chunk in enumerate(chunks):
        received = group_exchange(outbound, chunk, base, 1, 2 * index)
        base += len(chunk)
        rows = received.reshape(len(chunk) * capacity, model_width)
        gathered = lax.all_gather(rows, "inner", axis=0, tiled=True)
        partial_value = expert_part(gathered, gate_weight[0], up_weight[0], down_weight[0])
        summed = lax.psum_scatter(
            partial_value.astype(jnp.bfloat16), "inner", scatter_dimension=0, tiled=True
        )
        returned.append((summed.reshape(len(chunk), capacity, model_width), chunk, index))
    back = [group_exchange(z, chunk, 0, -1, 2 * index + 1) for z, chunk, index in returned]
    back_rows = jnp.concatenate(back, axis=0) if len(back) > 1 else back[0]
    expert_out = jnp.einsum(
        "gct,gcd->td",
        dispatch.reshape(groups, capacity, tok_count),
        back_rows,
        preferred_element_type=jnp.float32,
    )
    return (gate_scale[:, None] * expert_out).astype(jnp.bfloat16)


def solution(mesh):
    in_specs = (
        P(("group", "inner"), None),
        P(("group", "inner")),
        P(("group", "inner")),
        P("group", None, "inner"),
        P("group", None, "inner"),
        P("group", "inner", None),
    )
    out_specs = P(("group", "inner"), None)
    return jax.shard_map(body, mesh=mesh, in_specs=in_specs, out_specs=out_specs, check_vma=False)
```

```python
import functools

import jax
import jax.numpy as jnp
from jax import lax
from jax.experimental import pallas as pl
from jax.experimental.pallas import tpu as pltpu
from jax.sharding import PartitionSpec as P

MESH = pl.DeviceIdType.MESH


def torus_sides(groups):
    side = 4 if groups % 4 == 0 and groups > 4 else groups
    return groups // side, side


def chunk_orders(groups):
    if groups == 16:
        return [
            [(0, 0), (0, 1), (0, 3), (2, 0)],
            [(0, 2), (2, 2), (1, 3), (3, 1)],
            [(1, 2), (3, 2), (2, 1), (2, 3)],
            [(1, 0), (3, 0), (1, 1), (3, 3)],
        ]
    pairs = [((0, k), (0, groups - k)) for k in range(1, (groups + 1) // 2)]
    first = [(0, 0)] + ([(0, groups // 2)] if groups % 2 == 0 and groups > 1 else [])
    second = []
    for index, pair in enumerate(pairs):
        (first if index < len(pairs) // 2 else second).extend(pair)
    return [first, second] if second else [first]


def peer_of(me, offset, sign, groups):
    rows, side = torus_sides(groups)
    dz, dy = offset
    z = lax.rem(me // side + sign * dz + rows, rows)
    y = lax.rem(lax.rem(me, side) + sign * dy + side, side)
    return z * side + y


def exchange_kernel(groups, offsets, src_base, sign, x_ref, y_ref, local_sem, send_sem, recv_sem):
    me = lax.axis_index("group")
    inner = lax.axis_index("inner")
    peers = [k for k in offsets if k != (0, 0)]
    barrier = pltpu.get_barrier_semaphore()
    for k in peers:
        pl.semaphore_signal(
            barrier, inc=1, device_id=(peer_of(me, k, 1, groups), inner), device_id_type=MESH
        )
    if peers:
        pl.semaphore_wait(barrier, len(peers))
    local = None
    sends = []
    for i, k in enumerate(offsets):
        if k == (0, 0):
            local = pltpu.make_async_copy(x_ref.at[src_base + i], y_ref.at[i], local_sem)
            local.start()
            continue
        dest = peer_of(me, k, sign, groups)
        copy = pltpu.make_async_remote_copy(
            src_ref=x_ref.at[src_base + i],
            dst_ref=y_ref.at[i],
            send_sem=send_sem.at[i],
            recv_sem=recv_sem.at[i],
            device_id=(dest, inner),
            device_id_type=MESH,
        )
        copy.start()
        sends.append(copy)
    for copy in sends:
        copy.wait_send()
    for i, k in enumerate(offsets):
        if k == (0, 0):
            continue
        source = peer_of(me, k, -sign, groups)
        pltpu.make_async_remote_copy(
            src_ref=x_ref.at[src_base + i],
            dst_ref=y_ref.at[i],
            send_sem=send_sem.at[i],
            recv_sem=recv_sem.at[i],
            device_id=(source, inner),
            device_id_type=MESH,
        ).wait_recv()
    if local is not None:
        local.wait()


def group_exchange(x, offsets, src_base, sign, collective_id):
    groups = lax.axis_size("group")
    count = len(offsets)
    return pl.pallas_call(
        functools.partial(exchange_kernel, groups, tuple(offsets), src_base, sign),
        out_shape=jax.ShapeDtypeStruct((count,) + x.shape[1:], x.dtype),
        in_specs=[pl.BlockSpec(memory_space=pl.ANY)],
        out_specs=pl.BlockSpec(memory_space=pl.ANY),
        scratch_shapes=[
            pltpu.SemaphoreType.DMA,
            pltpu.SemaphoreType.DMA((count,)),
            pltpu.SemaphoreType.DMA((count,)),
        ],
        compiler_params=pltpu.CompilerParams(collective_id=collective_id, has_side_effects=True),
    )(x)


def expert_part(rows_in, gate_mat, up_mat, down_mat):
    gate_pre = jnp.dot(rows_in, gate_mat, preferred_element_type=jnp.float32)
    up_pre = jnp.dot(rows_in, up_mat, preferred_element_type=jnp.float32)
    hidden = (jax.nn.silu(gate_pre) * up_pre).astype(jnp.bfloat16)
    return jnp.dot(hidden, down_mat, preferred_element_type=jnp.float32)


def body(tokens, target, gate_scale, gate_weight, up_weight, down_weight):
    groups = lax.axis_size("group")
    tok_count = tokens.shape[0]
    model_width = tokens.shape[1]
    capacity = tok_count * 5 // (4 * groups)
    slot_count = groups * capacity
    chunks = chunk_orders(groups)
    order = [k for chunk in chunks for k in chunk]
    rows, side = torus_sides(groups)
    position_of = [0] * groups
    for position, (dz, dy) in enumerate(order):
        position_of[dz * side + dy] = position
    me = lax.axis_index("group")
    onehot = (target[:, None] == jnp.arange(groups, dtype=jnp.int32)[None, :]).astype(jnp.int32)
    rank_in = jnp.sum((jnp.cumsum(onehot, axis=0) - onehot) * onehot, axis=1)
    relative_z = lax.rem(target // side - me // side + rows, rows)
    relative_y = lax.rem(lax.rem(target, side) - lax.rem(me, side) + side, side)
    relative = jnp.where(target < groups, relative_z * side + relative_y, 0)
    position = jnp.asarray(position_of, dtype=jnp.int32)[relative]
    slot_of = jnp.where(target < groups, position * capacity + rank_in, slot_count)
    dispatch = (slot_of[None, :] == jnp.arange(slot_count, dtype=jnp.int32)[:, None]).astype(
        jnp.bfloat16
    )
    outbound = jnp.dot(dispatch, tokens, preferred_element_type=jnp.float32).astype(jnp.bfloat16)
    outbound = outbound.reshape(groups, capacity, model_width)
    returned = []
    base = 0
    for index, chunk in enumerate(chunks):
        received = group_exchange(outbound, chunk, base, 1, 2 * index)
        base += len(chunk)
        rows = received.reshape(len(chunk) * capacity, model_width)
        gathered = lax.all_gather(rows, "inner", axis=0, tiled=True)
        partial_value = expert_part(gathered, gate_weight[0], up_weight[0], down_weight[0])
        summed = lax.psum_scatter(
            partial_value.astype(jnp.bfloat16), "inner", scatter_dimension=0, tiled=True
        )
        returned.append((summed.reshape(len(chunk), capacity, model_width), chunk, index))
    back = [group_exchange(z, chunk, 0, -1, 2 * index + 1) for z, chunk, index in returned]
    back_rows = jnp.concatenate(back, axis=0) if len(back) > 1 else back[0]
    expert_out = jnp.einsum(
        "gct,gcd->td",
        dispatch.reshape(groups, capacity, tok_count),
        back_rows,
        preferred_element_type=jnp.float32,
    )
    return (gate_scale[:, None] * expert_out).astype(jnp.bfloat16)


def solution(mesh):
    in_specs = (
        P(("group", "inner"), None),
        P(("group", "inner")),
        P(("group", "inner")),
        P("group", None, "inner"),
        P("group", None, "inner"),
        P("group", "inner", None),
    )
    out_specs = P(("group", "inner"), None)
    return jax.shard_map(body, mesh=mesh, in_specs=in_specs, out_specs=out_specs, check_vma=False)
```

```python
import functools

import jax
import jax.numpy as jnp
from jax import lax
from jax.experimental import pallas as pl
from jax.experimental.pallas import tpu as pltpu
from jax.sharding import PartitionSpec as P

MESH = pl.DeviceIdType.MESH


def torus_sides(groups):
    side = 4 if groups % 4 == 0 and groups > 4 else groups
    return groups // side, side


def chunk_orders(groups):
    if groups == 16:
        return [
            [(0, 0), (0, 1), (0, 3), (0, 2)],
            [(1, 1), (3, 3), (1, 3), (3, 1), (1, 2), (3, 2), (2, 1), (2, 3)],
            [(1, 0), (3, 0), (2, 0), (2, 2)],
        ]
    pairs = [((0, k), (0, groups - k)) for k in range(1, (groups + 1) // 2)]
    first = [(0, 0)] + ([(0, groups // 2)] if groups % 2 == 0 and groups > 1 else [])
    second = []
    for index, pair in enumerate(pairs):
        (first if index < len(pairs) // 2 else second).extend(pair)
    return [first, second] if second else [first]


def peer_of(me, offset, sign, groups):
    rows, side = torus_sides(groups)
    dz, dy = offset
    z = lax.rem(me // side + sign * dz + rows, rows)
    y = lax.rem(lax.rem(me, side) + sign * dy + side, side)
    return z * side + y


def exchange_kernel(groups, offsets, src_base, sign, x_ref, y_ref, local_sem, send_sem, recv_sem):
    me = lax.axis_index("group")
    inner = lax.axis_index("inner")
    peers = [k for k in offsets if k != (0, 0)]
    barrier = pltpu.get_barrier_semaphore()
    for k in peers:
        pl.semaphore_signal(
            barrier, inc=1, device_id=(peer_of(me, k, 1, groups), inner), device_id_type=MESH
        )
    if peers:
        pl.semaphore_wait(barrier, len(peers))
    local = None
    sends = []
    for i, k in enumerate(offsets):
        if k == (0, 0):
            local = pltpu.make_async_copy(x_ref.at[src_base + i], y_ref.at[i], local_sem)
            local.start()
            continue
        dest = peer_of(me, k, sign, groups)
        copy = pltpu.make_async_remote_copy(
            src_ref=x_ref.at[src_base + i],
            dst_ref=y_ref.at[i],
            send_sem=send_sem.at[i],
            recv_sem=recv_sem.at[i],
            device_id=(dest, inner),
            device_id_type=MESH,
        )
        copy.start()
        sends.append(copy)
    for copy in sends:
        copy.wait_send()
    for i, k in enumerate(offsets):
        if k == (0, 0):
            continue
        source = peer_of(me, k, -sign, groups)
        pltpu.make_async_remote_copy(
            src_ref=x_ref.at[src_base + i],
            dst_ref=y_ref.at[i],
            send_sem=send_sem.at[i],
            recv_sem=recv_sem.at[i],
            device_id=(source, inner),
            device_id_type=MESH,
        ).wait_recv()
    if local is not None:
        local.wait()


def group_exchange(x, offsets, src_base, sign, collective_id):
    groups = lax.axis_size("group")
    count = len(offsets)
    return pl.pallas_call(
        functools.partial(exchange_kernel, groups, tuple(offsets), src_base, sign),
        out_shape=jax.ShapeDtypeStruct((count,) + x.shape[1:], x.dtype),
        in_specs=[pl.BlockSpec(memory_space=pl.ANY)],
        out_specs=pl.BlockSpec(memory_space=pl.ANY),
        scratch_shapes=[
            pltpu.SemaphoreType.DMA,
            pltpu.SemaphoreType.DMA((count,)),
            pltpu.SemaphoreType.DMA((count,)),
        ],
        compiler_params=pltpu.CompilerParams(collective_id=collective_id, has_side_effects=True),
    )(x)


def expert_part(rows_in, gate_mat, up_mat, down_mat):
    gate_pre = jnp.dot(rows_in, gate_mat, preferred_element_type=jnp.float32)
    up_pre = jnp.dot(rows_in, up_mat, preferred_element_type=jnp.float32)
    hidden = (jax.nn.silu(gate_pre) * up_pre).astype(jnp.bfloat16)
    return jnp.dot(hidden, down_mat, preferred_element_type=jnp.float32)


def body(tokens, target, gate_scale, gate_weight, up_weight, down_weight):
    groups = lax.axis_size("group")
    tok_count = tokens.shape[0]
    model_width = tokens.shape[1]
    capacity = tok_count * 5 // (4 * groups)
    slot_count = groups * capacity
    chunks = chunk_orders(groups)
    order = [k for chunk in chunks for k in chunk]
    rows, side = torus_sides(groups)
    position_of = [0] * groups
    for position, (dz, dy) in enumerate(order):
        position_of[dz * side + dy] = position
    me = lax.axis_index("group")
    onehot = (target[:, None] == jnp.arange(groups, dtype=jnp.int32)[None, :]).astype(jnp.int32)
    rank_in = jnp.sum((jnp.cumsum(onehot, axis=0) - onehot) * onehot, axis=1)
    relative_z = lax.rem(target // side - me // side + rows, rows)
    relative_y = lax.rem(lax.rem(target, side) - lax.rem(me, side) + side, side)
    relative = jnp.where(target < groups, relative_z * side + relative_y, 0)
    position = jnp.asarray(position_of, dtype=jnp.int32)[relative]
    slot_of = jnp.where(target < groups, position * capacity + rank_in, slot_count)
    dispatch = (slot_of[None, :] == jnp.arange(slot_count, dtype=jnp.int32)[:, None]).astype(
        jnp.bfloat16
    )
    outbound = jnp.dot(dispatch, tokens, preferred_element_type=jnp.float32).astype(jnp.bfloat16)
    lanes = 128 if (capacity * model_width) % 128 == 0 else model_width
    slab = (capacity * model_width // lanes, lanes)
    outbound = outbound.reshape((groups,) + slab)
    returned = []
    base = 0
    for index, chunk in enumerate(chunks):
        received = group_exchange(outbound, chunk, base, 1, 2 * index)
        base += len(chunk)
        rows = received.reshape(len(chunk) * capacity, model_width)
        gathered = lax.all_gather(rows, "inner", axis=0, tiled=True)
        partial_value = expert_part(gathered, gate_weight[0], up_weight[0], down_weight[0])
        summed = lax.psum_scatter(
            partial_value.astype(jnp.bfloat16), "inner", scatter_dimension=0, tiled=True
        )
        returned.append((summed.reshape((len(chunk),) + slab), chunk, index))
    back = [group_exchange(z, chunk, 0, -1, 2 * index + 1) for z, chunk, index in returned]
    back_rows = jnp.concatenate(back, axis=0) if len(back) > 1 else back[0]
    back_rows = back_rows.reshape(groups, capacity, model_width)
    expert_out = jnp.einsum(
        "gct,gcd->td",
        dispatch.reshape(groups, capacity, tok_count),
        back_rows,
        preferred_element_type=jnp.float32,
    )
    return (gate_scale[:, None] * expert_out).astype(jnp.bfloat16)


def solution(mesh):
    in_specs = (
        P(("group", "inner"), None),
        P(("group", "inner")),
        P(("group", "inner")),
        P("group", None, "inner"),
        P("group", None, "inner"),
        P("group", "inner", None),
    )
    out_specs = P(("group", "inner"), None)
    return jax.shard_map(body, mesh=mesh, in_specs=in_specs, out_specs=out_specs, check_vma=False)
```

```python
import functools

import jax
import jax.numpy as jnp
from jax import lax
from jax.experimental import pallas as pl
from jax.experimental.pallas import tpu as pltpu
from jax.sharding import PartitionSpec as P

MESH = pl.DeviceIdType.MESH


def torus_sides(groups):
    side = 4 if groups % 4 == 0 and groups > 4 else groups
    return groups // side, side


def chunk_orders(groups):
    if groups == 16:
        return [
            [(0, 0), (0, 1), (0, 3), (1, 0), (3, 0), (1, 2), (3, 2), (2, 2)],
            [(0, 2), (2, 0), (1, 1), (3, 3), (1, 3), (3, 1), (2, 1), (2, 3)],
        ]
    pairs = [((0, k), (0, groups - k)) for k in range(1, (groups + 1) // 2)]
    first = [(0, 0)] + ([(0, groups // 2)] if groups % 2 == 0 and groups > 1 else [])
    second = []
    for index, pair in enumerate(pairs):
        (first if index < len(pairs) // 2 else second).extend(pair)
    return [first, second] if second else [first]


def peer_of(me, offset, sign, groups):
    rows, side = torus_sides(groups)
    dz, dy = offset
    z = lax.rem(me // side + sign * dz + rows, rows)
    y = lax.rem(lax.rem(me, side) + sign * dy + side, side)
    return z * side + y


def exchange_kernel(groups, offsets, src_base, sign, x_ref, y_ref, local_sem, send_sem, recv_sem):
    me = lax.axis_index("group")
    inner = lax.axis_index("inner")
    peers = [k for k in offsets if k != (0, 0)]
    barrier = pltpu.get_barrier_semaphore()
    for k in peers:
        pl.semaphore_signal(
            barrier, inc=1, device_id=(peer_of(me, k, 1, groups), inner), device_id_type=MESH
        )
    if peers:
        pl.semaphore_wait(barrier, len(peers))
    local = None
    sends = []
    for i, k in enumerate(offsets):
        if k == (0, 0):
            local = pltpu.make_async_copy(x_ref.at[src_base + i], y_ref.at[i], local_sem)
            local.start()
            continue
        dest = peer_of(me, k, sign, groups)
        copy = pltpu.make_async_remote_copy(
            src_ref=x_ref.at[src_base + i],
            dst_ref=y_ref.at[i],
            send_sem=send_sem.at[i],
            recv_sem=recv_sem.at[i],
            device_id=(dest, inner),
            device_id_type=MESH,
        )
        copy.start()
        sends.append(copy)
    for copy in sends:
        copy.wait_send()
    for i, k in enumerate(offsets):
        if k == (0, 0):
            continue
        source = peer_of(me, k, -sign, groups)
        pltpu.make_async_remote_copy(
            src_ref=x_ref.at[src_base + i],
            dst_ref=y_ref.at[i],
            send_sem=send_sem.at[i],
            recv_sem=recv_sem.at[i],
            device_id=(source, inner),
            device_id_type=MESH,
        ).wait_recv()
    if local is not None:
        local.wait()


def group_exchange(x, offsets, src_base, sign, collective_id):
    groups = lax.axis_size("group")
    count = len(offsets)
    return pl.pallas_call(
        functools.partial(exchange_kernel, groups, tuple(offsets), src_base, sign),
        out_shape=jax.ShapeDtypeStruct((count,) + x.shape[1:], x.dtype),
        in_specs=[pl.BlockSpec(memory_space=pl.ANY)],
        out_specs=pl.BlockSpec(memory_space=pl.ANY),
        scratch_shapes=[
            pltpu.SemaphoreType.DMA,
            pltpu.SemaphoreType.DMA((count,)),
            pltpu.SemaphoreType.DMA((count,)),
        ],
        compiler_params=pltpu.CompilerParams(collective_id=collective_id, has_side_effects=True),
    )(x)


def expert_part(rows_in, gate_mat, up_mat, down_mat):
    gate_pre = jnp.dot(rows_in, gate_mat, preferred_element_type=jnp.float32)
    up_pre = jnp.dot(rows_in, up_mat, preferred_element_type=jnp.float32)
    hidden = (jax.nn.silu(gate_pre) * up_pre).astype(jnp.bfloat16)
    return jnp.dot(hidden, down_mat, preferred_element_type=jnp.float32)


def body(tokens, target, gate_scale, gate_weight, up_weight, down_weight):
    groups = lax.axis_size("group")
    tok_count = tokens.shape[0]
    model_width = tokens.shape[1]
    capacity = tok_count * 5 // (4 * groups)
    slot_count = groups * capacity
    chunks = chunk_orders(groups)
    order = [k for chunk in chunks for k in chunk]
    rows, side = torus_sides(groups)
    position_of = [0] * groups
    for position, (dz, dy) in enumerate(order):
        position_of[dz * side + dy] = position
    me = lax.axis_index("group")
    onehot = (target[:, None] == jnp.arange(groups, dtype=jnp.int32)[None, :]).astype(jnp.int32)
    rank_in = jnp.sum((jnp.cumsum(onehot, axis=0) - onehot) * onehot, axis=1)
    relative_z = lax.rem(target // side - me // side + rows, rows)
    relative_y = lax.rem(lax.rem(target, side) - lax.rem(me, side) + side, side)
    relative = jnp.where(target < groups, relative_z * side + relative_y, 0)
    position = jnp.asarray(position_of, dtype=jnp.int32)[relative]
    slot_of = jnp.where(target < groups, position * capacity + rank_in, slot_count)
    dispatch = (slot_of[None, :] == jnp.arange(slot_count, dtype=jnp.int32)[:, None]).astype(
        jnp.bfloat16
    )
    outbound = jnp.dot(dispatch, tokens, preferred_element_type=jnp.float32).astype(jnp.bfloat16)
    lanes = 128 if (capacity * model_width) % 128 == 0 else model_width
    slab = (capacity * model_width // lanes, lanes)
    outbound = outbound.reshape((groups,) + slab)
    returned = []
    base = 0
    for index, chunk in enumerate(chunks):
        received = group_exchange(outbound, chunk, base, 1, 2 * index)
        base += len(chunk)
        rows = received.reshape(len(chunk) * capacity, model_width)
        gathered = lax.all_gather(rows, "inner", axis=0, tiled=True)
        partial_value = expert_part(gathered, gate_weight[0], up_weight[0], down_weight[0])
        summed = lax.psum_scatter(
            partial_value.astype(jnp.bfloat16), "inner", scatter_dimension=0, tiled=True
        )
        returned.append((summed.reshape((len(chunk),) + slab), chunk, index))
    back = [group_exchange(z, chunk, 0, -1, 2 * index + 1) for z, chunk, index in returned]
    back_rows = jnp.concatenate(back, axis=0) if len(back) > 1 else back[0]
    back_rows = back_rows.reshape(groups, capacity, model_width)
    expert_out = jnp.einsum(
        "gct,gcd->td",
        dispatch.reshape(groups, capacity, tok_count),
        back_rows,
        preferred_element_type=jnp.float32,
    )
    return (gate_scale[:, None] * expert_out).astype(jnp.bfloat16)


def solution(mesh):
    in_specs = (
        P(("group", "inner"), None),
        P(("group", "inner")),
        P(("group", "inner")),
        P("group", None, "inner"),
        P("group", None, "inner"),
        P("group", "inner", None),
    )
    out_specs = P(("group", "inner"), None)
    return jax.shard_map(body, mesh=mesh, in_specs=in_specs, out_specs=out_specs, check_vma=False)
```

```python
import functools

import jax
import jax.numpy as jnp
from jax import lax
from jax.experimental import pallas as pl
from jax.experimental.pallas import tpu as pltpu
from jax.sharding import PartitionSpec as P

MESH = pl.DeviceIdType.MESH


def torus_sides(groups):
    side = 4 if groups % 4 == 0 and groups > 4 else groups
    return groups // side, side


def chunk_orders(groups):
    if groups == 16:
        return [
            [(0, 0), (0, 1), (0, 3), (1, 0), (3, 0), (1, 2), (3, 2), (2, 2)],
            [(0, 2), (2, 0), (1, 1), (3, 3), (1, 3), (3, 1), (2, 1), (2, 3)],
        ]
    pairs = [((0, k), (0, groups - k)) for k in range(1, (groups + 1) // 2)]
    first = [(0, 0)] + ([(0, groups // 2)] if groups % 2 == 0 and groups > 1 else [])
    second = []
    for index, pair in enumerate(pairs):
        (first if index < len(pairs) // 2 else second).extend(pair)
    return [first, second] if second else [first]


def peer_of(me, offset, sign, groups):
    rows, side = torus_sides(groups)
    dz, dy = offset
    z = lax.rem(me // side + sign * dz + rows, rows)
    y = lax.rem(lax.rem(me, side) + sign * dy + side, side)
    return z * side + y


def exchange_kernel(groups, offsets, src_base, sign, x_ref, y_ref, local_sem, send_sem, recv_sem):
    me = lax.axis_index("group")
    inner = lax.axis_index("inner")
    peers = [k for k in offsets if k != (0, 0)]
    barrier = pltpu.get_barrier_semaphore()
    for k in peers:
        pl.semaphore_signal(
            barrier, inc=1, device_id=(peer_of(me, k, 1, groups), inner), device_id_type=MESH
        )
    if peers:
        pl.semaphore_wait(barrier, len(peers))
    local = None
    sends = []
    for i, k in enumerate(offsets):
        if k == (0, 0):
            local = pltpu.make_async_copy(x_ref.at[src_base + i], y_ref.at[i], local_sem)
            local.start()
            continue
        dest = peer_of(me, k, sign, groups)
        copy = pltpu.make_async_remote_copy(
            src_ref=x_ref.at[src_base + i],
            dst_ref=y_ref.at[i],
            send_sem=send_sem.at[i],
            recv_sem=recv_sem.at[i],
            device_id=(dest, inner),
            device_id_type=MESH,
        )
        copy.start()
        sends.append(copy)
    for copy in sends:
        copy.wait_send()
    for i, k in enumerate(offsets):
        if k == (0, 0):
            continue
        source = peer_of(me, k, -sign, groups)
        pltpu.make_async_remote_copy(
            src_ref=x_ref.at[src_base + i],
            dst_ref=y_ref.at[i],
            send_sem=send_sem.at[i],
            recv_sem=recv_sem.at[i],
            device_id=(source, inner),
            device_id_type=MESH,
        ).wait_recv()
    if local is not None:
        local.wait()


def group_exchange(x, offsets, src_base, sign, collective_id):
    groups = lax.axis_size("group")
    count = len(offsets)
    return pl.pallas_call(
        functools.partial(exchange_kernel, groups, tuple(offsets), src_base, sign),
        out_shape=jax.ShapeDtypeStruct((count,) + x.shape[1:], x.dtype),
        in_specs=[pl.BlockSpec(memory_space=pl.ANY)],
        out_specs=pl.BlockSpec(memory_space=pl.ANY),
        scratch_shapes=[
            pltpu.SemaphoreType.DMA,
            pltpu.SemaphoreType.DMA((count,)),
            pltpu.SemaphoreType.DMA((count,)),
        ],
        compiler_params=pltpu.CompilerParams(collective_id=collective_id, has_side_effects=True),
    )(x)


def partner_kernel(swap, x_ref, y_ref, local_sem, send_sem, recv_sem):
    group = lax.axis_index("group")
    inner = lax.axis_index("inner")
    core = lax.rem(inner, 2)
    partner = inner + 1 - 2 * core
    barrier = pltpu.get_barrier_semaphore()
    pl.semaphore_signal(barrier, inc=1, device_id=(group, partner), device_id_type=MESH)
    pl.semaphore_wait(barrier, 1)
    if swap:
        src, dst, mine = x_ref.at[1 - core], y_ref, None
        theirs = y_ref
    else:
        src, dst = x_ref, y_ref.at[core]
        mine = pltpu.make_async_copy(x_ref, y_ref.at[core], local_sem)
        mine.start()
        theirs = y_ref.at[1 - core]
    copy = pltpu.make_async_remote_copy(
        src_ref=src,
        dst_ref=dst,
        send_sem=send_sem,
        recv_sem=recv_sem,
        device_id=(group, partner),
        device_id_type=MESH,
    )
    copy.start()
    copy.wait_send()
    pltpu.make_async_remote_copy(
        src_ref=src,
        dst_ref=theirs,
        send_sem=send_sem,
        recv_sem=recv_sem,
        device_id=(group, partner),
        device_id_type=MESH,
    ).wait_recv()
    if mine is not None:
        mine.wait()


def partner_exchange(x, swap, collective_id):
    shape = x.shape[1:] if swap else (2,) + x.shape
    return pl.pallas_call(
        functools.partial(partner_kernel, swap),
        out_shape=jax.ShapeDtypeStruct(shape, x.dtype),
        in_specs=[pl.BlockSpec(memory_space=pl.ANY)],
        out_specs=pl.BlockSpec(memory_space=pl.ANY),
        scratch_shapes=[
            pltpu.SemaphoreType.DMA,
            pltpu.SemaphoreType.DMA,
            pltpu.SemaphoreType.DMA,
        ],
        compiler_params=pltpu.CompilerParams(collective_id=collective_id, has_side_effects=True),
    )(x)


def expert_part(rows_in, gate_mat, up_mat, down_mat):
    gate_pre = jnp.dot(rows_in, gate_mat, preferred_element_type=jnp.float32)
    up_pre = jnp.dot(rows_in, up_mat, preferred_element_type=jnp.float32)
    hidden = (jax.nn.silu(gate_pre) * up_pre).astype(jnp.bfloat16)
    return jnp.dot(hidden, down_mat, preferred_element_type=jnp.float32)


def body(tokens, target, gate_scale, gate_weight, up_weight, down_weight):
    groups = lax.axis_size("group")
    inner_size = lax.axis_size("inner")
    tok_count = tokens.shape[0]
    model_width = tokens.shape[1]
    capacity = tok_count * 5 // (4 * groups)
    slot_count = groups * capacity
    chunks = chunk_orders(groups)
    order = [k for chunk in chunks for k in chunk]
    rows, side = torus_sides(groups)
    position_of = [0] * groups
    for position, (dz, dy) in enumerate(order):
        position_of[dz * side + dy] = position
    me = lax.axis_index("group")
    onehot = (target[:, None] == jnp.arange(groups, dtype=jnp.int32)[None, :]).astype(jnp.int32)
    rank_in = jnp.sum((jnp.cumsum(onehot, axis=0) - onehot) * onehot, axis=1)
    relative_z = lax.rem(target // side - me // side + rows, rows)
    relative_y = lax.rem(lax.rem(target, side) - lax.rem(me, side) + side, side)
    relative = jnp.where(target < groups, relative_z * side + relative_y, 0)
    position = jnp.asarray(position_of, dtype=jnp.int32)[relative]
    slot_of = jnp.where(target < groups, position * capacity + rank_in, slot_count)
    dispatch = (slot_of[None, :] == jnp.arange(slot_count, dtype=jnp.int32)[:, None]).astype(
        jnp.bfloat16
    )
    outbound = jnp.dot(dispatch, tokens, preferred_element_type=jnp.float32).astype(jnp.bfloat16)
    lanes = 128 if (capacity * model_width) % 128 == 0 else model_width
    slab = (capacity * model_width // lanes, lanes)
    outbound = outbound.reshape((groups,) + slab)
    returned = []
    base = 0
    for index, chunk in enumerate(chunks):
        received = group_exchange(outbound, chunk, base, 1, 2 * index)
        base += len(chunk)
        rows = received.reshape(len(chunk) * capacity, model_width)
        same_core = [list(range(c, inner_size, 2)) for c in range(2)]
        core = lax.rem(lax.axis_index("inner"), 2)
        mine = lax.all_gather(rows, "inner", axis=0, tiled=True, axis_index_groups=same_core)
        gathered = partner_exchange(mine, False, 8 + 4 * index).reshape(-1, model_width)
        partial_value = expert_part(gathered, gate_weight[0], up_weight[0], down_weight[0])
        partial_value = partial_value.astype(jnp.bfloat16).reshape((2, -1, model_width))
        received_sum = partner_exchange(partial_value, True, 9 + 4 * index)
        own_part = lax.dynamic_index_in_dim(partial_value, core, axis=0, keepdims=False)
        pair_sum = (own_part.astype(jnp.float32) + received_sum.astype(jnp.float32)).astype(
            jnp.bfloat16
        )
        summed = lax.psum_scatter(
            pair_sum, "inner", scatter_dimension=0, tiled=True, axis_index_groups=same_core
        )
        returned.append((summed.reshape((len(chunk),) + slab), chunk, index))
    back = [group_exchange(z, chunk, 0, -1, 2 * index + 1) for z, chunk, index in returned]
    back_rows = jnp.concatenate(back, axis=0) if len(back) > 1 else back[0]
    back_rows = back_rows.reshape(groups, capacity, model_width)
    expert_out = jnp.einsum(
        "gct,gcd->td",
        dispatch.reshape(groups, capacity, tok_count),
        back_rows,
        preferred_element_type=jnp.float32,
    )
    return (gate_scale[:, None] * expert_out).astype(jnp.bfloat16)


def solution(mesh):
    in_specs = (
        P(("group", "inner"), None),
        P(("group", "inner")),
        P(("group", "inner")),
        P("group", None, "inner"),
        P("group", None, "inner"),
        P("group", "inner", None),
    )
    out_specs = P(("group", "inner"), None)
    return jax.shard_map(body, mesh=mesh, in_specs=in_specs, out_specs=out_specs, check_vma=False)
```

```python
import functools

import jax
import jax.numpy as jnp
from jax import lax
from jax.experimental import pallas as pl
from jax.experimental.pallas import tpu as pltpu
from jax.sharding import PartitionSpec as P

MESH = pl.DeviceIdType.MESH


def torus_sides(groups):
    side = 4 if groups % 4 == 0 and groups > 4 else groups
    return groups // side, side


def chunk_orders(groups):
    if groups == 16:
        return [
            [(0, 0), (0, 1), (0, 3), (1, 0), (3, 0), (1, 2), (3, 2), (2, 2)],
            [(0, 2), (2, 0), (1, 1), (3, 3), (1, 3), (3, 1), (2, 1), (2, 3)],
        ]
    pairs = [((0, k), (0, groups - k)) for k in range(1, (groups + 1) // 2)]
    first = [(0, 0)] + ([(0, groups // 2)] if groups % 2 == 0 and groups > 1 else [])
    second = []
    for index, pair in enumerate(pairs):
        (first if index < len(pairs) // 2 else second).extend(pair)
    return [first, second] if second else [first]


def peer_of(me, offset, sign, groups):
    rows, side = torus_sides(groups)
    dz, dy = offset
    z = lax.rem(me // side + sign * dz + rows, rows)
    y = lax.rem(lax.rem(me, side) + sign * dy + side, side)
    return z * side + y


def exchange_kernel(groups, offsets, src_base, sign, x_ref, y_ref, local_sem, send_sem, recv_sem):
    me = lax.axis_index("group")
    inner = lax.axis_index("inner")
    peers = [k for k in offsets if k != (0, 0)]
    barrier = pltpu.get_barrier_semaphore()
    for k in peers:
        pl.semaphore_signal(
            barrier, inc=1, device_id=(peer_of(me, k, 1, groups), inner), device_id_type=MESH
        )
    if peers:
        pl.semaphore_wait(barrier, len(peers))
    local = None
    sends = []
    for i, k in enumerate(offsets):
        if k == (0, 0):
            local = pltpu.make_async_copy(x_ref.at[src_base + i], y_ref.at[i], local_sem)
            local.start()
            continue
        dest = peer_of(me, k, sign, groups)
        copy = pltpu.make_async_remote_copy(
            src_ref=x_ref.at[src_base + i],
            dst_ref=y_ref.at[i],
            send_sem=send_sem.at[i],
            recv_sem=recv_sem.at[i],
            device_id=(dest, inner),
            device_id_type=MESH,
        )
        copy.start()
        sends.append(copy)
    for copy in sends:
        copy.wait_send()
    for i, k in enumerate(offsets):
        if k == (0, 0):
            continue
        source = peer_of(me, k, -sign, groups)
        pltpu.make_async_remote_copy(
            src_ref=x_ref.at[src_base + i],
            dst_ref=y_ref.at[i],
            send_sem=send_sem.at[i],
            recv_sem=recv_sem.at[i],
            device_id=(source, inner),
            device_id_type=MESH,
        ).wait_recv()
    if local is not None:
        local.wait()


def group_exchange(x, offsets, src_base, sign, collective_id):
    groups = lax.axis_size("group")
    count = len(offsets)
    return pl.pallas_call(
        functools.partial(exchange_kernel, groups, tuple(offsets), src_base, sign),
        out_shape=jax.ShapeDtypeStruct((count,) + x.shape[1:], x.dtype),
        in_specs=[pl.BlockSpec(memory_space=pl.ANY)],
        out_specs=pl.BlockSpec(memory_space=pl.ANY),
        scratch_shapes=[
            pltpu.SemaphoreType.DMA,
            pltpu.SemaphoreType.DMA((count,)),
            pltpu.SemaphoreType.DMA((count,)),
        ],
        compiler_params=pltpu.CompilerParams(collective_id=collective_id, has_side_effects=True),
    )(x)


def gather_kernel(chips, x_ref, y_ref, send_sem, recv_sem):
    group = lax.axis_index("group")
    inner = lax.axis_index("inner")
    core = lax.rem(inner, 2)
    chip = inner // 2
    partner = inner + 1 - 2 * core
    barrier = pltpu.get_barrier_semaphore()
    others = [lax.rem(chip + d, chips) for d in range(1, chips)]
    for other in others:
        pl.semaphore_signal(
            barrier, inc=1, device_id=(group, 2 * other + core), device_id_type=MESH
        )
    pl.semaphore_signal(barrier, inc=1, device_id=(group, partner), device_id_type=MESH)
    pl.semaphore_wait(barrier, chips)

    def copy_to(src, slot, device, index):
        return pltpu.make_async_remote_copy(
            src_ref=src,
            dst_ref=y_ref.at[slot],
            send_sem=send_sem.at[index],
            recv_sem=recv_sem.at[slot],
            device_id=(group, device),
            device_id_type=MESH,
        )

    direct = []
    for d, other in enumerate(others):
        copy = copy_to(x_ref, inner, 2 * other + core, d)
        copy.start()
        direct.append(copy)
    to_partner = copy_to(x_ref, inner, partner, chips - 1)
    to_partner.start()
    forwards = []
    for d, other in enumerate(others):
        slot = 2 * other + core
        copy_to(x_ref, slot, 2 * other + core, d).wait_recv()
        forward = copy_to(y_ref.at[slot], slot, partner, chips + d)
        forward.start()
        forwards.append(forward)
    for copy in direct:
        copy.wait_send()
    to_partner.wait_send()
    copy_to(x_ref, partner, partner, chips - 1).wait_recv()
    for d, other in enumerate(others):
        slot = 2 * other + 1 - core
        copy_to(x_ref, slot, partner, chips + d).wait_recv()
    for forward in forwards:
        forward.wait_send()


def inner_gather(x, collective_id):
    inner_size = lax.axis_size("inner")
    chips = inner_size // 2
    out = pl.pallas_call(
        functools.partial(gather_kernel, chips),
        out_shape=jax.ShapeDtypeStruct((inner_size,) + x.shape, x.dtype),
        in_specs=[pl.BlockSpec(memory_space=pl.ANY)],
        out_specs=pl.BlockSpec(memory_space=pl.ANY),
        scratch_shapes=[
            pltpu.SemaphoreType.DMA((2 * chips,)),
            pltpu.SemaphoreType.DMA((inner_size,)),
        ],
        compiler_params=pltpu.CompilerParams(collective_id=collective_id, has_side_effects=True),
    )(x)
    out = lax.dynamic_update_index_in_dim(out, x, lax.axis_index("inner"), axis=0)
    return out.reshape((-1,) + x.shape[1:])


def expert_part(rows_in, gate_mat, up_mat, down_mat):
    gate_pre = jnp.dot(rows_in, gate_mat, preferred_element_type=jnp.float32)
    up_pre = jnp.dot(rows_in, up_mat, preferred_element_type=jnp.float32)
    hidden = (jax.nn.silu(gate_pre) * up_pre).astype(jnp.bfloat16)
    return jnp.dot(hidden, down_mat, preferred_element_type=jnp.float32)


def body(tokens, target, gate_scale, gate_weight, up_weight, down_weight):
    groups = lax.axis_size("group")
    tok_count = tokens.shape[0]
    model_width = tokens.shape[1]
    capacity = tok_count * 5 // (4 * groups)
    slot_count = groups * capacity
    chunks = chunk_orders(groups)
    order = [k for chunk in chunks for k in chunk]
    rows, side = torus_sides(groups)
    position_of = [0] * groups
    for position, (dz, dy) in enumerate(order):
        position_of[dz * side + dy] = position
    me = lax.axis_index("group")
    onehot = (target[:, None] == jnp.arange(groups, dtype=jnp.int32)[None, :]).astype(jnp.int32)
    rank_in = jnp.sum((jnp.cumsum(onehot, axis=0) - onehot) * onehot, axis=1)
    relative_z = lax.rem(target // side - me // side + rows, rows)
    relative_y = lax.rem(lax.rem(target, side) - lax.rem(me, side) + side, side)
    relative = jnp.where(target < groups, relative_z * side + relative_y, 0)
    position = jnp.asarray(position_of, dtype=jnp.int32)[relative]
    slot_of = jnp.where(target < groups, position * capacity + rank_in, slot_count)
    dispatch = (slot_of[None, :] == jnp.arange(slot_count, dtype=jnp.int32)[:, None]).astype(
        jnp.bfloat16
    )
    outbound = jnp.dot(dispatch, tokens, preferred_element_type=jnp.float32).astype(jnp.bfloat16)
    lanes = 128 if (capacity * model_width) % 128 == 0 else model_width
    slab = (capacity * model_width // lanes, lanes)
    outbound = outbound.reshape((groups,) + slab)
    returned = []
    base = 0
    for index, chunk in enumerate(chunks):
        received = group_exchange(outbound, chunk, base, 1, 2 * index)
        base += len(chunk)
        rows = received.reshape(len(chunk) * capacity, model_width)
        if index == len(chunks) - 1 and lax.axis_size("inner") % 2 == 0:
            gathered = inner_gather(rows, 8)
        else:
            gathered = lax.all_gather(rows, "inner", axis=0, tiled=True)
        partial_value = expert_part(gathered, gate_weight[0], up_weight[0], down_weight[0])
        summed = lax.psum_scatter(
            partial_value.astype(jnp.bfloat16), "inner", scatter_dimension=0, tiled=True
        )
        returned.append((summed.reshape((len(chunk),) + slab), chunk, index))
    back = [group_exchange(z, chunk, 0, -1, 2 * index + 1) for z, chunk, index in returned]
    back_rows = jnp.concatenate(back, axis=0) if len(back) > 1 else back[0]
    back_rows = back_rows.reshape(groups, capacity, model_width)
    expert_out = jnp.einsum(
        "gct,gcd->td",
        dispatch.reshape(groups, capacity, tok_count),
        back_rows,
        preferred_element_type=jnp.float32,
    )
    return (gate_scale[:, None] * expert_out).astype(jnp.bfloat16)


def solution(mesh):
    in_specs = (
        P(("group", "inner"), None),
        P(("group", "inner")),
        P(("group", "inner")),
        P("group", None, "inner"),
        P("group", None, "inner"),
        P("group", "inner", None),
    )
    out_specs = P(("group", "inner"), None)
    return jax.shard_map(body, mesh=mesh, in_specs=in_specs, out_specs=out_specs, check_vma=False)
```

```python
import functools

import jax
import jax.numpy as jnp
from jax import lax
from jax.experimental import pallas as pl
from jax.experimental.pallas import tpu as pltpu
from jax.sharding import PartitionSpec as P

MESH = pl.DeviceIdType.MESH


def torus_sides(groups):
    side = 4 if groups % 4 == 0 and groups > 4 else groups
    return groups // side, side


def chunk_orders(groups):
    if groups == 16:
        return [
            [(0, 0), (0, 1), (0, 3), (1, 0), (3, 0), (1, 2), (3, 2), (2, 2)],
            [(0, 2), (2, 0), (1, 1), (3, 3), (1, 3), (3, 1), (2, 1), (2, 3)],
        ]
    pairs = [((0, k), (0, groups - k)) for k in range(1, (groups + 1) // 2)]
    first = [(0, 0)] + ([(0, groups // 2)] if groups % 2 == 0 and groups > 1 else [])
    second = []
    for index, pair in enumerate(pairs):
        (first if index < len(pairs) // 2 else second).extend(pair)
    return [first, second] if second else [first]


def peer_of(me, offset, sign, groups):
    rows, side = torus_sides(groups)
    dz, dy = offset
    z = lax.rem(me // side + sign * dz + rows, rows)
    y = lax.rem(lax.rem(me, side) + sign * dy + side, side)
    return z * side + y


def exchange_kernel(groups, offsets, src_base, sign, x_ref, y_ref, local_sem, send_sem, recv_sem):
    me = lax.axis_index("group")
    inner = lax.axis_index("inner")
    peers = [k for k in offsets if k != (0, 0)]
    barrier = pltpu.get_barrier_semaphore()
    for k in peers:
        pl.semaphore_signal(
            barrier, inc=1, device_id=(peer_of(me, k, 1, groups), inner), device_id_type=MESH
        )
    if peers:
        pl.semaphore_wait(barrier, len(peers))
    local = None
    sends = []
    for i, k in enumerate(offsets):
        if k == (0, 0):
            local = pltpu.make_async_copy(x_ref.at[src_base + i], y_ref.at[i], local_sem)
            local.start()
            continue
        dest = peer_of(me, k, sign, groups)
        copy = pltpu.make_async_remote_copy(
            src_ref=x_ref.at[src_base + i],
            dst_ref=y_ref.at[i],
            send_sem=send_sem.at[i],
            recv_sem=recv_sem.at[i],
            device_id=(dest, inner),
            device_id_type=MESH,
        )
        copy.start()
        sends.append(copy)
    for copy in sends:
        copy.wait_send()
    for i, k in enumerate(offsets):
        if k == (0, 0):
            continue
        source = peer_of(me, k, -sign, groups)
        pltpu.make_async_remote_copy(
            src_ref=x_ref.at[src_base + i],
            dst_ref=y_ref.at[i],
            send_sem=send_sem.at[i],
            recv_sem=recv_sem.at[i],
            device_id=(source, inner),
            device_id_type=MESH,
        ).wait_recv()
    if local is not None:
        local.wait()


def group_exchange(x, offsets, src_base, sign, collective_id):
    groups = lax.axis_size("group")
    count = len(offsets)
    return pl.pallas_call(
        functools.partial(exchange_kernel, groups, tuple(offsets), src_base, sign),
        out_shape=jax.ShapeDtypeStruct((count,) + x.shape[1:], x.dtype),
        in_specs=[pl.BlockSpec(memory_space=pl.ANY)],
        out_specs=pl.BlockSpec(memory_space=pl.ANY),
        scratch_shapes=[
            pltpu.SemaphoreType.DMA,
            pltpu.SemaphoreType.DMA((count,)),
            pltpu.SemaphoreType.DMA((count,)),
        ],
        compiler_params=pltpu.CompilerParams(collective_id=collective_id, has_side_effects=True),
    )(x)


def expert_part(rows_in, gate_mat, up_mat, down_mat):
    gate_pre = jnp.dot(rows_in, gate_mat, preferred_element_type=jnp.float32)
    up_pre = jnp.dot(rows_in, up_mat, preferred_element_type=jnp.float32)
    hidden = (jax.nn.silu(gate_pre) * up_pre).astype(jnp.bfloat16)
    return jnp.dot(hidden, down_mat, preferred_element_type=jnp.float32)


def body(tokens, target, gate_scale, gate_weight, up_weight, down_weight):
    groups = lax.axis_size("group")
    tok_count = tokens.shape[0]
    model_width = tokens.shape[1]
    capacity = tok_count * 5 // (4 * groups)
    slot_count = groups * capacity
    chunks = chunk_orders(groups)
    order = [k for chunk in chunks for k in chunk]
    rows, side = torus_sides(groups)
    position_of = [0] * groups
    for position, (dz, dy) in enumerate(order):
        position_of[dz * side + dy] = position
    me = lax.axis_index("group")
    onehot = (target[:, None] == jnp.arange(groups, dtype=jnp.int32)[None, :]).astype(jnp.int32)
    rank_in = jnp.sum((jnp.cumsum(onehot, axis=0) - onehot) * onehot, axis=1)
    relative_z = lax.rem(target // side - me // side + rows, rows)
    relative_y = lax.rem(lax.rem(target, side) - lax.rem(me, side) + side, side)
    relative = jnp.where(target < groups, relative_z * side + relative_y, 0)
    position = jnp.asarray(position_of, dtype=jnp.int32)[relative]
    slot_of = jnp.where(target < groups, position * capacity + rank_in, slot_count)
    dispatch = (slot_of[None, :] == jnp.arange(slot_count, dtype=jnp.int32)[:, None]).astype(
        jnp.bfloat16
    )
    outbound = jnp.dot(dispatch, tokens, preferred_element_type=jnp.float32).astype(jnp.bfloat16)
    lanes = 128 if (capacity * model_width) % 128 == 0 else model_width
    slab = (capacity * model_width // lanes, lanes)
    returned = []
    base = 0
    for index, chunk in enumerate(chunks):
        piece = outbound[base * capacity : (base + len(chunk)) * capacity]
        received = group_exchange(piece.reshape((len(chunk),) + slab), chunk, 0, 1, 2 * index)
        base += len(chunk)
        rows = received.reshape(len(chunk) * capacity, model_width)
        gathered = lax.all_gather(rows, "inner", axis=0, tiled=True)
        partial_value = expert_part(gathered, gate_weight[0], up_weight[0], down_weight[0])
        summed = lax.psum_scatter(
            partial_value.astype(jnp.bfloat16), "inner", scatter_dimension=0, tiled=True
        )
        returned.append((summed.reshape((len(chunk),) + slab), chunk, index))
    expert_out = None
    base = 0
    for z, chunk, index in returned:
        back_rows = group_exchange(z, chunk, 0, -1, 2 * index + 1)
        term = jnp.einsum(
            "gct,gcd->td",
            dispatch[base * capacity : (base + len(chunk)) * capacity].reshape(
                len(chunk), capacity, tok_count
            ),
            back_rows.reshape(len(chunk), capacity, model_width),
            preferred_element_type=jnp.float32,
        )
        base += len(chunk)
        expert_out = term if expert_out is None else expert_out + term
    return (gate_scale[:, None] * expert_out).astype(jnp.bfloat16)


def solution(mesh):
    in_specs = (
        P(("group", "inner"), None),
        P(("group", "inner")),
        P(("group", "inner")),
        P("group", None, "inner"),
        P("group", None, "inner"),
        P("group", "inner", None),
    )
    out_specs = P(("group", "inner"), None)
    return jax.shard_map(body, mesh=mesh, in_specs=in_specs, out_specs=out_specs, check_vma=False)
```

```python
import functools

import jax
import jax.numpy as jnp
from jax import lax
from jax.experimental import pallas as pl
from jax.experimental.pallas import tpu as pltpu
from jax.sharding import PartitionSpec as P

MESH = pl.DeviceIdType.MESH


def torus_sides(groups):
    side = 4 if groups % 4 == 0 and groups > 4 else groups
    return groups // side, side


def chunk_orders(groups):
    if groups == 16:
        return [
            [(0, 0), (0, 1), (0, 3), (1, 0), (3, 0), (1, 2), (3, 2), (2, 2)],
            [(0, 2), (2, 0), (1, 1), (3, 3), (1, 3), (3, 1), (2, 1), (2, 3)],
        ]
    pairs = [((0, k), (0, groups - k)) for k in range(1, (groups + 1) // 2)]
    first = [(0, 0)] + ([(0, groups // 2)] if groups % 2 == 0 and groups > 1 else [])
    second = []
    for index, pair in enumerate(pairs):
        (first if index < len(pairs) // 2 else second).extend(pair)
    return [first, second] if second else [first]


def peer_of(me, offset, sign, groups):
    rows, side = torus_sides(groups)
    dz, dy = offset
    z = lax.rem(me // side + sign * dz + rows, rows)
    y = lax.rem(lax.rem(me, side) + sign * dy + side, side)
    return z * side + y


def exchange_kernel(groups, offsets, src_base, sign, x_ref, y_ref, local_sem, send_sem, recv_sem):
    me = lax.axis_index("group")
    inner = lax.axis_index("inner")
    peers = [k for k in offsets if k != (0, 0)]
    barrier = pltpu.get_barrier_semaphore()
    for k in peers:
        pl.semaphore_signal(
            barrier, inc=1, device_id=(peer_of(me, k, 1, groups), inner), device_id_type=MESH
        )
    if peers:
        pl.semaphore_wait(barrier, len(peers))
    local = None
    sends = []
    for i, k in enumerate(offsets):
        if k == (0, 0):
            local = pltpu.make_async_copy(x_ref.at[src_base + i], y_ref.at[i], local_sem)
            local.start()
            continue
        dest = peer_of(me, k, sign, groups)
        copy = pltpu.make_async_remote_copy(
            src_ref=x_ref.at[src_base + i],
            dst_ref=y_ref.at[i],
            send_sem=send_sem.at[i],
            recv_sem=recv_sem.at[i],
            device_id=(dest, inner),
            device_id_type=MESH,
        )
        copy.start()
        sends.append(copy)
    for copy in sends:
        copy.wait_send()
    for i, k in enumerate(offsets):
        if k == (0, 0):
            continue
        source = peer_of(me, k, -sign, groups)
        pltpu.make_async_remote_copy(
            src_ref=x_ref.at[src_base + i],
            dst_ref=y_ref.at[i],
            send_sem=send_sem.at[i],
            recv_sem=recv_sem.at[i],
            device_id=(source, inner),
            device_id_type=MESH,
        ).wait_recv()
    if local is not None:
        local.wait()


def group_exchange(x, offsets, src_base, sign, collective_id):
    groups = lax.axis_size("group")
    count = len(offsets)
    return pl.pallas_call(
        functools.partial(exchange_kernel, groups, tuple(offsets), src_base, sign),
        out_shape=jax.ShapeDtypeStruct((count,) + x.shape[1:], x.dtype),
        in_specs=[pl.BlockSpec(memory_space=pl.ANY)],
        out_specs=pl.BlockSpec(memory_space=pl.ANY),
        scratch_shapes=[
            pltpu.SemaphoreType.DMA,
            pltpu.SemaphoreType.DMA((count,)),
            pltpu.SemaphoreType.DMA((count,)),
        ],
        compiler_params=pltpu.CompilerParams(collective_id=collective_id, has_side_effects=True),
    )(x)


def swap_kernel(x_ref, y_ref, send_sem, recv_sem):
    group = lax.axis_index("group")
    inner = lax.axis_index("inner")
    core = lax.rem(inner, 2)
    partner = inner + 1 - 2 * core
    barrier = pltpu.get_barrier_semaphore()
    pl.semaphore_signal(barrier, inc=1, device_id=(group, partner), device_id_type=MESH)
    pl.semaphore_wait(barrier, 1)
    copy = pltpu.make_async_remote_copy(
        src_ref=x_ref.at[:, 1 - core],
        dst_ref=y_ref,
        send_sem=send_sem,
        recv_sem=recv_sem,
        device_id=(group, partner),
        device_id_type=MESH,
    )
    copy.start()
    copy.wait_send()
    copy.wait_recv()


def partner_swap(x, collective_id):
    return pl.pallas_call(
        swap_kernel,
        out_shape=jax.ShapeDtypeStruct(x.shape[:1] + x.shape[2:], x.dtype),
        in_specs=[pl.BlockSpec(memory_space=pl.ANY)],
        out_specs=pl.BlockSpec(memory_space=pl.ANY),
        scratch_shapes=[pltpu.SemaphoreType.DMA, pltpu.SemaphoreType.DMA],
        compiler_params=pltpu.CompilerParams(collective_id=collective_id, has_side_effects=True),
    )(x)


def expert_part(rows_in, gate_mat, up_mat, down_mat):
    gate_pre = jnp.dot(rows_in, gate_mat, preferred_element_type=jnp.float32)
    up_pre = jnp.dot(rows_in, up_mat, preferred_element_type=jnp.float32)
    hidden = (jax.nn.silu(gate_pre) * up_pre).astype(jnp.bfloat16)
    return jnp.dot(hidden, down_mat, preferred_element_type=jnp.float32)


def body(tokens, target, gate_scale, gate_weight, up_weight, down_weight):
    groups = lax.axis_size("group")
    tok_count = tokens.shape[0]
    model_width = tokens.shape[1]
    capacity = tok_count * 5 // (4 * groups)
    slot_count = groups * capacity
    chunks = chunk_orders(groups)
    order = [k for chunk in chunks for k in chunk]
    rows, side = torus_sides(groups)
    position_of = [0] * groups
    for position, (dz, dy) in enumerate(order):
        position_of[dz * side + dy] = position
    me = lax.axis_index("group")
    onehot = (target[:, None] == jnp.arange(groups, dtype=jnp.int32)[None, :]).astype(jnp.int32)
    rank_in = jnp.sum((jnp.cumsum(onehot, axis=0) - onehot) * onehot, axis=1)
    relative_z = lax.rem(target // side - me // side + rows, rows)
    relative_y = lax.rem(lax.rem(target, side) - lax.rem(me, side) + side, side)
    relative = jnp.where(target < groups, relative_z * side + relative_y, 0)
    position = jnp.asarray(position_of, dtype=jnp.int32)[relative]
    slot_of = jnp.where(target < groups, position * capacity + rank_in, slot_count)
    dispatch = (slot_of[None, :] == jnp.arange(slot_count, dtype=jnp.int32)[:, None]).astype(
        jnp.bfloat16
    )
    outbound = jnp.dot(dispatch, tokens, preferred_element_type=jnp.float32).astype(jnp.bfloat16)
    lanes = 128 if (capacity * model_width) % 128 == 0 else model_width
    slab = (capacity * model_width // lanes, lanes)
    returned = []
    base = 0
    for index, chunk in enumerate(chunks):
        piece = outbound[base * capacity : (base + len(chunk)) * capacity]
        received = group_exchange(piece.reshape((len(chunk),) + slab), chunk, 0, 1, 2 * index)
        base += len(chunk)
        rows = received.reshape(len(chunk) * capacity, model_width)
        gathered = lax.all_gather(rows, "inner", axis=0, tiled=True)
        partial_value = expert_part(gathered, gate_weight[0], up_weight[0], down_weight[0])
        inner_size = lax.axis_size("inner")
        if inner_size % 2 == 0:
            same_core = [list(range(c, inner_size, 2)) for c in range(2)]
            core = lax.rem(lax.axis_index("inner"), 2)
            by_core = partial_value.astype(jnp.bfloat16).reshape(inner_size // 2, 2, -1, model_width)
            received_sum = partner_swap(by_core, 8 + index)
            own_part = lax.dynamic_index_in_dim(by_core, core, axis=1, keepdims=False)
            pair_sum = own_part.astype(jnp.float32) + received_sum.astype(jnp.float32)
            summed = lax.psum_scatter(
                pair_sum.astype(jnp.bfloat16).reshape(-1, model_width),
                "inner",
                scatter_dimension=0,
                tiled=True,
                axis_index_groups=same_core,
            )
        else:
            summed = lax.psum_scatter(
                partial_value.astype(jnp.bfloat16), "inner", scatter_dimension=0, tiled=True
            )
        returned.append((summed.reshape((len(chunk),) + slab), chunk, index))
    expert_out = None
    base = 0
    for z, chunk, index in returned:
        back_rows = group_exchange(z, chunk, 0, -1, 2 * index + 1)
        term = jnp.einsum(
            "gct,gcd->td",
            dispatch[base * capacity : (base + len(chunk)) * capacity].reshape(
                len(chunk), capacity, tok_count
            ),
            back_rows.reshape(len(chunk), capacity, model_width),
            preferred_element_type=jnp.float32,
        )
        base += len(chunk)
        expert_out = term if expert_out is None else expert_out + term
    return (gate_scale[:, None] * expert_out).astype(jnp.bfloat16)


def solution(mesh):
    in_specs = (
        P(("group", "inner"), None),
        P(("group", "inner")),
        P(("group", "inner")),
        P("group", None, "inner"),
        P("group", None, "inner"),
        P("group", "inner", None),
    )
    out_specs = P(("group", "inner"), None)
    return jax.shard_map(body, mesh=mesh, in_specs=in_specs, out_specs=out_specs, check_vma=False)
```

```python
import functools

import jax
import jax.numpy as jnp
from jax import lax
from jax.experimental import pallas as pl
from jax.experimental.pallas import tpu as pltpu
from jax.sharding import PartitionSpec as P

MESH = pl.DeviceIdType.MESH


def torus_sides(groups):
    side = 4 if groups % 4 == 0 and groups > 4 else groups
    return groups // side, side


def chunk_orders(groups):
    if groups == 16:
        return [
            [(0, 0), (0, 1), (0, 3), (1, 0), (3, 0), (1, 2), (3, 2), (2, 2)],
            [(0, 2), (2, 0), (1, 1), (3, 3), (1, 3), (3, 1), (2, 1), (2, 3)],
        ]
    pairs = [((0, k), (0, groups - k)) for k in range(1, (groups + 1) // 2)]
    first = [(0, 0)] + ([(0, groups // 2)] if groups % 2 == 0 and groups > 1 else [])
    second = []
    for index, pair in enumerate(pairs):
        (first if index < len(pairs) // 2 else second).extend(pair)
    return [first, second] if second else [first]


def peer_of(me, offset, sign, groups):
    rows, side = torus_sides(groups)
    dz, dy = offset
    z = lax.rem(me // side + sign * dz + rows, rows)
    y = lax.rem(lax.rem(me, side) + sign * dy + side, side)
    return z * side + y


def exchange_kernel(groups, offsets, src_base, sign, x_ref, y_ref, local_sem, send_sem, recv_sem):
    me = lax.axis_index("group")
    inner = lax.axis_index("inner")
    peers = [k for k in offsets if k != (0, 0)]
    barrier = pltpu.get_barrier_semaphore()
    for k in peers:
        pl.semaphore_signal(
            barrier, inc=1, device_id=(peer_of(me, k, 1, groups), inner), device_id_type=MESH
        )
    if peers:
        pl.semaphore_wait(barrier, len(peers))
    local = None
    sends = []
    for i, k in enumerate(offsets):
        if k == (0, 0):
            local = pltpu.make_async_copy(x_ref.at[src_base + i], y_ref.at[i], local_sem)
            local.start()
            continue
        dest = peer_of(me, k, sign, groups)
        copy = pltpu.make_async_remote_copy(
            src_ref=x_ref.at[src_base + i],
            dst_ref=y_ref.at[i],
            send_sem=send_sem.at[i],
            recv_sem=recv_sem.at[i],
            device_id=(dest, inner),
            device_id_type=MESH,
        )
        copy.start()
        sends.append(copy)
    for copy in sends:
        copy.wait_send()
    for i, k in enumerate(offsets):
        if k == (0, 0):
            continue
        source = peer_of(me, k, -sign, groups)
        pltpu.make_async_remote_copy(
            src_ref=x_ref.at[src_base + i],
            dst_ref=y_ref.at[i],
            send_sem=send_sem.at[i],
            recv_sem=recv_sem.at[i],
            device_id=(source, inner),
            device_id_type=MESH,
        ).wait_recv()
    if local is not None:
        local.wait()


def group_exchange(x, offsets, src_base, sign, collective_id):
    groups = lax.axis_size("group")
    count = len(offsets)
    return pl.pallas_call(
        functools.partial(exchange_kernel, groups, tuple(offsets), src_base, sign),
        out_shape=jax.ShapeDtypeStruct((count,) + x.shape[1:], x.dtype),
        in_specs=[pl.BlockSpec(memory_space=pl.ANY)],
        out_specs=pl.BlockSpec(memory_space=pl.ANY),
        scratch_shapes=[
            pltpu.SemaphoreType.DMA,
            pltpu.SemaphoreType.DMA((count,)),
            pltpu.SemaphoreType.DMA((count,)),
        ],
        compiler_params=pltpu.CompilerParams(collective_id=collective_id, has_side_effects=True),
    )(x)


def swap_kernel(x_ref, y_ref, send_sem, recv_sem):
    group = lax.axis_index("group")
    inner = lax.axis_index("inner")
    core = lax.rem(inner, 2)
    partner = inner + 1 - 2 * core
    barrier = pltpu.get_barrier_semaphore()
    pl.semaphore_signal(barrier, inc=1, device_id=(group, partner), device_id_type=MESH)
    pl.semaphore_wait(barrier, 1)
    copy = pltpu.make_async_remote_copy(
        src_ref=x_ref.at[:, 1 - core],
        dst_ref=y_ref,
        send_sem=send_sem,
        recv_sem=recv_sem,
        device_id=(group, partner),
        device_id_type=MESH,
    )
    copy.start()
    copy.wait_send()
    copy.wait_recv()


def partner_swap(x, collective_id):
    return pl.pallas_call(
        swap_kernel,
        out_shape=jax.ShapeDtypeStruct(x.shape[:1] + x.shape[2:], x.dtype),
        in_specs=[pl.BlockSpec(memory_space=pl.ANY)],
        out_specs=pl.BlockSpec(memory_space=pl.ANY),
        scratch_shapes=[pltpu.SemaphoreType.DMA, pltpu.SemaphoreType.DMA],
        compiler_params=pltpu.CompilerParams(collective_id=collective_id, has_side_effects=True),
    )(x)


def expert_part(rows_in, gate_mat, up_mat, down_mat):
    gate_pre = jnp.dot(rows_in, gate_mat, preferred_element_type=jnp.float32)
    up_pre = jnp.dot(rows_in, up_mat, preferred_element_type=jnp.float32)
    hidden = (jax.nn.silu(gate_pre) * up_pre).astype(jnp.bfloat16)
    return jnp.dot(hidden, down_mat, preferred_element_type=jnp.float32)


def body(tokens, target, gate_scale, gate_weight, up_weight, down_weight):
    groups = lax.axis_size("group")
    tok_count = tokens.shape[0]
    model_width = tokens.shape[1]
    capacity = tok_count * 5 // (4 * groups)
    slot_count = groups * capacity
    chunks = chunk_orders(groups)
    order = [k for chunk in chunks for k in chunk]
    rows, side = torus_sides(groups)
    position_of = [0] * groups
    for position, (dz, dy) in enumerate(order):
        position_of[dz * side + dy] = position
    me = lax.axis_index("group")
    onehot = (target[:, None] == jnp.arange(groups, dtype=jnp.int32)[None, :]).astype(jnp.int32)
    rank_in = jnp.sum((jnp.cumsum(onehot, axis=0) - onehot) * onehot, axis=1)
    relative_z = lax.rem(target // side - me // side + rows, rows)
    relative_y = lax.rem(lax.rem(target, side) - lax.rem(me, side) + side, side)
    relative = jnp.where(target < groups, relative_z * side + relative_y, 0)
    position = jnp.asarray(position_of, dtype=jnp.int32)[relative]
    slot_of = jnp.where(target < groups, position * capacity + rank_in, slot_count)
    dispatch = (slot_of[None, :] == jnp.arange(slot_count, dtype=jnp.int32)[:, None]).astype(
        jnp.bfloat16
    )
    outbound = jnp.dot(dispatch, tokens, preferred_element_type=jnp.float32).astype(jnp.bfloat16)
    lanes = 128 if (capacity * model_width) % 128 == 0 else model_width
    slab = (capacity * model_width // lanes, lanes)
    returned = []
    base = 0
    inner_size = lax.axis_size("inner")
    weights = (gate_weight[0], up_weight[0], down_weight[0])
    for index, chunk in enumerate(chunks):
        local_first = index == 0 and chunk[0] == (0, 0) and inner_size % 2 == 0
        remote = chunk[1:] if local_first else chunk
        piece = outbound[(base + len(chunk) - len(remote)) * capacity : (base + len(chunk)) * capacity]
        received = group_exchange(piece.reshape((len(remote),) + slab), remote, 0, 1, 2 * index)
        rows = received.reshape(len(remote) * capacity, model_width)
        gathered = lax.all_gather(rows, "inner", axis=0, tiled=True)
        partial_value = expert_part(gathered, *weights).astype(jnp.bfloat16)
        if local_first:
            local_rows = lax.all_gather(
                outbound[base * capacity : (base + 1) * capacity], "inner", axis=0, tiled=True
            )
            local_value = expert_part(local_rows, *weights).astype(jnp.bfloat16)
            partial_value = jnp.concatenate(
                [
                    local_value.reshape(inner_size, capacity, model_width),
                    partial_value.reshape(inner_size, len(remote) * capacity, model_width),
                ],
                axis=1,
            )
        partial_value = partial_value.reshape(-1, model_width)
        base += len(chunk)
        if inner_size % 2 == 0:
            same_core = [list(range(c, inner_size, 2)) for c in range(2)]
            core = lax.rem(lax.axis_index("inner"), 2)
            by_core = partial_value.reshape(inner_size // 2, 2, -1, model_width)
            received_sum = partner_swap(by_core, 8 + index)
            own_part = lax.dynamic_index_in_dim(by_core, core, axis=1, keepdims=False)
            pair_sum = own_part.astype(jnp.float32) + received_sum.astype(jnp.float32)
            summed = lax.psum_scatter(
                pair_sum.astype(jnp.bfloat16).reshape(-1, model_width),
                "inner",
                scatter_dimension=0,
                tiled=True,
                axis_index_groups=same_core,
            )
        else:
            summed = lax.psum_scatter(partial_value, "inner", scatter_dimension=0, tiled=True)
        returned.append((summed.reshape((len(chunk),) + slab), chunk, index))
    expert_out = None
    base = 0
    for z, chunk, index in returned:
        back_rows = group_exchange(z, chunk, 0, -1, 2 * index + 1)
        term = jnp.einsum(
            "gct,gcd->td",
            dispatch[base * capacity : (base + len(chunk)) * capacity].reshape(
                len(chunk), capacity, tok_count
            ),
            back_rows.reshape(len(chunk), capacity, model_width),
            preferred_element_type=jnp.float32,
        )
        base += len(chunk)
        expert_out = term if expert_out is None else expert_out + term
    return (gate_scale[:, None] * expert_out).astype(jnp.bfloat16)


def solution(mesh):
    in_specs = (
        P(("group", "inner"), None),
        P(("group", "inner")),
        P(("group", "inner")),
        P("group", None, "inner"),
        P("group", None, "inner"),
        P("group", "inner", None),
    )
    out_specs = P(("group", "inner"), None)
    return jax.shard_map(body, mesh=mesh, in_specs=in_specs, out_specs=out_specs, check_vma=False)
```

```python
import functools

import jax
import jax.numpy as jnp
from jax import lax
from jax.experimental import pallas as pl
from jax.experimental.pallas import tpu as pltpu
from jax.sharding import PartitionSpec as P

MESH = pl.DeviceIdType.MESH


def torus_sides(groups):
    side = 4 if groups % 4 == 0 and groups > 4 else groups
    return groups // side, side


def chunk_orders(groups):
    if groups == 16:
        return [
            [(0, 0), (0, 1), (0, 3), (1, 0), (3, 0), (1, 2), (3, 2), (2, 2)],
            [(0, 2), (2, 0), (1, 1), (3, 3), (1, 3), (3, 1), (2, 1), (2, 3)],
        ]
    pairs = [((0, k), (0, groups - k)) for k in range(1, (groups + 1) // 2)]
    first = [(0, 0)] + ([(0, groups // 2)] if groups % 2 == 0 and groups > 1 else [])
    second = []
    for index, pair in enumerate(pairs):
        (first if index < len(pairs) // 2 else second).extend(pair)
    return [first, second] if second else [first]


def peer_of(me, offset, sign, groups):
    rows, side = torus_sides(groups)
    dz, dy = offset
    z = lax.rem(me // side + sign * dz + rows, rows)
    y = lax.rem(lax.rem(me, side) + sign * dy + side, side)
    return z * side + y


def exchange_kernel(groups, offsets, src_base, sign, x_ref, y_ref, local_sem, send_sem, recv_sem):
    me = lax.axis_index("group")
    inner = lax.axis_index("inner")
    peers = [k for k in offsets if k != (0, 0)]
    barrier = pltpu.get_barrier_semaphore()
    for k in peers:
        pl.semaphore_signal(
            barrier, inc=1, device_id=(peer_of(me, k, 1, groups), inner), device_id_type=MESH
        )
    if peers:
        pl.semaphore_wait(barrier, len(peers))
    local = None
    sends = []
    for i, k in enumerate(offsets):
        if k == (0, 0):
            local = pltpu.make_async_copy(x_ref.at[src_base + i], y_ref.at[i], local_sem)
            local.start()
            continue
        dest = peer_of(me, k, sign, groups)
        copy = pltpu.make_async_remote_copy(
            src_ref=x_ref.at[src_base + i],
            dst_ref=y_ref.at[i],
            send_sem=send_sem.at[i],
            recv_sem=recv_sem.at[i],
            device_id=(dest, inner),
            device_id_type=MESH,
        )
        copy.start()
        sends.append(copy)
    for copy in sends:
        copy.wait_send()
    for i, k in enumerate(offsets):
        if k == (0, 0):
            continue
        source = peer_of(me, k, -sign, groups)
        pltpu.make_async_remote_copy(
            src_ref=x_ref.at[src_base + i],
            dst_ref=y_ref.at[i],
            send_sem=send_sem.at[i],
            recv_sem=recv_sem.at[i],
            device_id=(source, inner),
            device_id_type=MESH,
        ).wait_recv()
    if local is not None:
        local.wait()


def group_exchange(x, offsets, src_base, sign, collective_id):
    groups = lax.axis_size("group")
    count = len(offsets)
    return pl.pallas_call(
        functools.partial(exchange_kernel, groups, tuple(offsets), src_base, sign),
        out_shape=jax.ShapeDtypeStruct((count,) + x.shape[1:], x.dtype),
        in_specs=[pl.BlockSpec(memory_space=pl.ANY)],
        out_specs=pl.BlockSpec(memory_space=pl.ANY),
        scratch_shapes=[
            pltpu.SemaphoreType.DMA,
            pltpu.SemaphoreType.DMA((count,)),
            pltpu.SemaphoreType.DMA((count,)),
        ],
        compiler_params=pltpu.CompilerParams(collective_id=collective_id, has_side_effects=True),
    )(x)


def swap_kernel(x_ref, y_ref, send_sem, recv_sem):
    group = lax.axis_index("group")
    inner = lax.axis_index("inner")
    core = lax.rem(inner, 2)
    partner = inner + 1 - 2 * core
    barrier = pltpu.get_barrier_semaphore()
    pl.semaphore_signal(barrier, inc=1, device_id=(group, partner), device_id_type=MESH)
    pl.semaphore_wait(barrier, 1)
    copy = pltpu.make_async_remote_copy(
        src_ref=x_ref.at[:, 1 - core],
        dst_ref=y_ref,
        send_sem=send_sem,
        recv_sem=recv_sem,
        device_id=(group, partner),
        device_id_type=MESH,
    )
    copy.start()
    copy.wait_send()
    copy.wait_recv()


def partner_swap(x, collective_id):
    return pl.pallas_call(
        swap_kernel,
        out_shape=jax.ShapeDtypeStruct(x.shape[:1] + x.shape[2:], x.dtype),
        in_specs=[pl.BlockSpec(memory_space=pl.ANY)],
        out_specs=pl.BlockSpec(memory_space=pl.ANY),
        scratch_shapes=[pltpu.SemaphoreType.DMA, pltpu.SemaphoreType.DMA],
        compiler_params=pltpu.CompilerParams(collective_id=collective_id, has_side_effects=True),
    )(x)


def expert_part(rows_in, gate_mat, up_mat, down_mat):
    gate_pre = jnp.dot(rows_in, gate_mat, preferred_element_type=jnp.float32)
    up_pre = jnp.dot(rows_in, up_mat, preferred_element_type=jnp.float32)
    hidden = (jax.nn.silu(gate_pre) * up_pre).astype(jnp.bfloat16)
    return jnp.dot(hidden, down_mat, preferred_element_type=jnp.float32)


def body(tokens, target, gate_scale, gate_weight, up_weight, down_weight):
    groups = lax.axis_size("group")
    tok_count = tokens.shape[0]
    model_width = tokens.shape[1]
    capacity = tok_count * 5 // (4 * groups)
    slot_count = groups * capacity
    chunks = chunk_orders(groups)
    order = [k for chunk in chunks for k in chunk]
    rows, side = torus_sides(groups)
    position_of = [0] * groups
    for position, (dz, dy) in enumerate(order):
        position_of[dz * side + dy] = position
    me = lax.axis_index("group")
    onehot = (target[:, None] == jnp.arange(groups, dtype=jnp.int32)[None, :]).astype(jnp.int32)
    rank_in = jnp.sum((jnp.cumsum(onehot, axis=0) - onehot) * onehot, axis=1)
    relative_z = lax.rem(target // side - me // side + rows, rows)
    relative_y = lax.rem(lax.rem(target, side) - lax.rem(me, side) + side, side)
    relative = jnp.where(target < groups, relative_z * side + relative_y, 0)
    position = jnp.asarray(position_of, dtype=jnp.int32)[relative]
    slot_of = jnp.where(target < groups, position * capacity + rank_in, slot_count)
    dispatch = (slot_of[None, :] == jnp.arange(slot_count, dtype=jnp.int32)[:, None]).astype(
        jnp.bfloat16
    )
    outbound = jnp.dot(dispatch, tokens, preferred_element_type=jnp.float32).astype(jnp.bfloat16)
    lanes = 128 if (capacity * model_width) % 128 == 0 else model_width
    slab = (capacity * model_width // lanes, lanes)
    returned = []
    base = 0
    for index, chunk in enumerate(chunks):
        piece = outbound[base * capacity : (base + len(chunk)) * capacity]
        received = group_exchange(piece.reshape((len(chunk),) + slab), chunk, 0, 1, 2 * index)
        base += len(chunk)
        rows = received.reshape(len(chunk) * capacity, model_width)
        gathered = lax.all_gather(rows, "inner", axis=0, tiled=True)
        partial_value = expert_part(gathered, gate_weight[0], up_weight[0], down_weight[0])
        inner_size = lax.axis_size("inner")
        if inner_size % 2 == 0:
            same_core = [list(range(c, inner_size, 2)) for c in range(2)]
            core = lax.rem(lax.axis_index("inner"), 2)
            by_core = partial_value.astype(jnp.bfloat16).reshape(inner_size // 2, 2, -1, model_width)
            received_sum = partner_swap(by_core, 8 + index)
            own_part = lax.dynamic_index_in_dim(by_core, core, axis=1, keepdims=False)
            pair_sum = own_part.astype(jnp.float32) + received_sum.astype(jnp.float32)
            summed = lax.psum_scatter(
                pair_sum.astype(jnp.bfloat16).reshape((-1,) + slab),
                "inner",
                scatter_dimension=0,
                tiled=True,
                axis_index_groups=same_core,
            )
        else:
            summed = lax.psum_scatter(
                partial_value.astype(jnp.bfloat16), "inner", scatter_dimension=0, tiled=True
            )
        returned.append((summed.reshape((len(chunk),) + slab), chunk, index))
    expert_out = None
    base = 0
    for z, chunk, index in returned:
        back_rows = group_exchange(z, chunk, 0, -1, 2 * index + 1)
        term = jnp.einsum(
            "gct,gcd->td",
            dispatch[base * capacity : (base + len(chunk)) * capacity].reshape(
                len(chunk), capacity, tok_count
            ),
            back_rows.reshape(len(chunk), capacity, model_width),
            preferred_element_type=jnp.float32,
        )
        base += len(chunk)
        expert_out = term if expert_out is None else expert_out + term
    return (gate_scale[:, None] * expert_out).astype(jnp.bfloat16)


def solution(mesh):
    in_specs = (
        P(("group", "inner"), None),
        P(("group", "inner")),
        P(("group", "inner")),
        P("group", None, "inner"),
        P("group", None, "inner"),
        P("group", "inner", None),
    )
    out_specs = P(("group", "inner"), None)
    return jax.shard_map(body, mesh=mesh, in_specs=in_specs, out_specs=out_specs, check_vma=False)
```

```python
import functools

import jax
import jax.numpy as jnp
from jax import lax
from jax.experimental import pallas as pl
from jax.experimental.pallas import tpu as pltpu
from jax.sharding import PartitionSpec as P

MESH = pl.DeviceIdType.MESH


def torus_sides(groups):
    side = 4 if groups % 4 == 0 and groups > 4 else groups
    return groups // side, side


def chunk_orders(groups):
    if groups == 16:
        return [
            [(0, 0), (0, 1), (0, 3), (1, 0), (3, 0), (1, 2), (3, 2), (2, 2)],
            [(0, 2), (2, 0), (1, 1), (3, 3), (1, 3), (3, 1), (2, 1), (2, 3)],
        ]
    pairs = [((0, k), (0, groups - k)) for k in range(1, (groups + 1) // 2)]
    first = [(0, 0)] + ([(0, groups // 2)] if groups % 2 == 0 and groups > 1 else [])
    second = []
    for index, pair in enumerate(pairs):
        (first if index < len(pairs) // 2 else second).extend(pair)
    return [first, second] if second else [first]


def peer_of(me, offset, sign, groups):
    rows, side = torus_sides(groups)
    dz, dy = offset
    z = lax.rem(me // side + sign * dz + rows, rows)
    y = lax.rem(lax.rem(me, side) + sign * dy + side, side)
    return z * side + y


def exchange_kernel(groups, offsets, src_base, sign, x_ref, y_ref, local_sem, send_sem, recv_sem):
    me = lax.axis_index("group")
    inner = lax.axis_index("inner")
    peers = [k for k in offsets if k != (0, 0)]
    barrier = pltpu.get_barrier_semaphore()
    for k in peers:
        pl.semaphore_signal(
            barrier, inc=1, device_id=(peer_of(me, k, 1, groups), inner), device_id_type=MESH
        )
    if peers:
        pl.semaphore_wait(barrier, len(peers))
    local = None
    sends = []
    for i, k in enumerate(offsets):
        if k == (0, 0):
            local = pltpu.make_async_copy(x_ref.at[src_base + i], y_ref.at[i], local_sem)
            local.start()
            continue
        dest = peer_of(me, k, sign, groups)
        copy = pltpu.make_async_remote_copy(
            src_ref=x_ref.at[src_base + i],
            dst_ref=y_ref.at[i],
            send_sem=send_sem.at[i],
            recv_sem=recv_sem.at[i],
            device_id=(dest, inner),
            device_id_type=MESH,
        )
        copy.start()
        sends.append(copy)
    for copy in sends:
        copy.wait_send()
    for i, k in enumerate(offsets):
        if k == (0, 0):
            continue
        source = peer_of(me, k, -sign, groups)
        pltpu.make_async_remote_copy(
            src_ref=x_ref.at[src_base + i],
            dst_ref=y_ref.at[i],
            send_sem=send_sem.at[i],
            recv_sem=recv_sem.at[i],
            device_id=(source, inner),
            device_id_type=MESH,
        ).wait_recv()
    if local is not None:
        local.wait()


def group_exchange(x, offsets, src_base, sign, collective_id):
    groups = lax.axis_size("group")
    count = len(offsets)
    return pl.pallas_call(
        functools.partial(exchange_kernel, groups, tuple(offsets), src_base, sign),
        out_shape=jax.ShapeDtypeStruct((count,) + x.shape[1:], x.dtype),
        in_specs=[pl.BlockSpec(memory_space=pl.ANY)],
        out_specs=pl.BlockSpec(memory_space=pl.ANY),
        scratch_shapes=[
            pltpu.SemaphoreType.DMA,
            pltpu.SemaphoreType.DMA((count,)),
            pltpu.SemaphoreType.DMA((count,)),
        ],
        compiler_params=pltpu.CompilerParams(collective_id=collective_id, has_side_effects=True),
    )(x)


def swap_kernel(x_ref, y_ref, send_sem, recv_sem):
    group = lax.axis_index("group")
    inner = lax.axis_index("inner")
    core = lax.rem(inner, 2)
    partner = inner + 1 - 2 * core
    barrier = pltpu.get_barrier_semaphore()
    pl.semaphore_signal(barrier, inc=1, device_id=(group, partner), device_id_type=MESH)
    pl.semaphore_wait(barrier, 1)
    copy = pltpu.make_async_remote_copy(
        src_ref=x_ref.at[:, 1 - core],
        dst_ref=y_ref,
        send_sem=send_sem,
        recv_sem=recv_sem,
        device_id=(group, partner),
        device_id_type=MESH,
    )
    copy.start()
    copy.wait_send()
    copy.wait_recv()


def partner_swap(x, collective_id):
    return pl.pallas_call(
        swap_kernel,
        out_shape=jax.ShapeDtypeStruct(x.shape[:1] + x.shape[2:], x.dtype),
        in_specs=[pl.BlockSpec(memory_space=pl.ANY)],
        out_specs=pl.BlockSpec(memory_space=pl.ANY),
        scratch_shapes=[pltpu.SemaphoreType.DMA, pltpu.SemaphoreType.DMA],
        compiler_params=pltpu.CompilerParams(collective_id=collective_id, has_side_effects=True),
    )(x)


def expert_part(rows_in, gate_mat, up_mat, down_mat):
    gate_pre = jnp.dot(rows_in, gate_mat, preferred_element_type=jnp.float32)
    up_pre = jnp.dot(rows_in, up_mat, preferred_element_type=jnp.float32)
    hidden = (jax.nn.silu(gate_pre) * up_pre).astype(jnp.bfloat16)
    return jnp.dot(hidden, down_mat, preferred_element_type=jnp.float32)


def body(tokens, target, gate_scale, gate_weight, up_weight, down_weight):
    groups = lax.axis_size("group")
    tok_count = tokens.shape[0]
    model_width = tokens.shape[1]
    capacity = tok_count * 5 // (4 * groups)
    slot_count = groups * capacity
    chunks = chunk_orders(groups)
    order = [k for chunk in chunks for k in chunk]
    rows, side = torus_sides(groups)
    position_of = [0] * groups
    for position, (dz, dy) in enumerate(order):
        position_of[dz * side + dy] = position
    me = lax.axis_index("group")
    onehot = (target[:, None] == jnp.arange(groups, dtype=jnp.int32)[None, :]).astype(jnp.int32)
    rank_in = jnp.sum((jnp.cumsum(onehot, axis=0) - onehot) * onehot, axis=1)
    relative_z = lax.rem(target // side - me // side + rows, rows)
    relative_y = lax.rem(lax.rem(target, side) - lax.rem(me, side) + side, side)
    relative = jnp.where(target < groups, relative_z * side + relative_y, 0)
    position = jnp.asarray(position_of, dtype=jnp.int32)[relative]
    slot_of = jnp.where(target < groups, position * capacity + rank_in, slot_count)
    dispatch = (slot_of[None, :] == jnp.arange(slot_count, dtype=jnp.int32)[:, None]).astype(
        jnp.bfloat16
    )
    outbound = jnp.dot(dispatch, tokens, preferred_element_type=jnp.float32).astype(jnp.bfloat16)
    lanes = 128 if (capacity * model_width) % 128 == 0 else model_width
    slab = (capacity * model_width // lanes, lanes)
    returned = []
    base = 0
    for index, chunk in enumerate(chunks):
        piece = outbound[base * capacity : (base + len(chunk)) * capacity]
        received = group_exchange(piece.reshape((len(chunk),) + slab), chunk, 0, 1, 2 * index)
        base += len(chunk)
        gathered = lax.all_gather(received, "inner", axis=0, tiled=True)
        gathered = gathered.reshape(-1, model_width)
        partial_value = expert_part(gathered, gate_weight[0], up_weight[0], down_weight[0])
        inner_size = lax.axis_size("inner")
        if inner_size % 2 == 0:
            same_core = [list(range(c, inner_size, 2)) for c in range(2)]
            core = lax.rem(lax.axis_index("inner"), 2)
            by_core = partial_value.astype(jnp.bfloat16).reshape(inner_size // 2, 2, -1, model_width)
            received_sum = partner_swap(by_core, 8 + index)
            own_part = lax.dynamic_index_in_dim(by_core, core, axis=1, keepdims=False)
            pair_sum = own_part.astype(jnp.float32) + received_sum.astype(jnp.float32)
            summed = lax.psum_scatter(
                pair_sum.astype(jnp.bfloat16).reshape((-1,) + slab),
                "inner",
                scatter_dimension=0,
                tiled=True,
                axis_index_groups=same_core,
            )
        else:
            summed = lax.psum_scatter(
                partial_value.astype(jnp.bfloat16), "inner", scatter_dimension=0, tiled=True
            )
        returned.append((summed.reshape((len(chunk),) + slab), chunk, index))
    expert_out = None
    base = 0
    for z, chunk, index in returned:
        back_rows = group_exchange(z, chunk, 0, -1, 2 * index + 1)
        term = jnp.einsum(
            "gct,gcd->td",
            dispatch[base * capacity : (base + len(chunk)) * capacity].reshape(
                len(chunk), capacity, tok_count
            ),
            back_rows.reshape(len(chunk), capacity, model_width),
            preferred_element_type=jnp.float32,
        )
        base += len(chunk)
        expert_out = term if expert_out is None else expert_out + term
    return (gate_scale[:, None] * expert_out).astype(jnp.bfloat16)


def solution(mesh):
    in_specs = (
        P(("group", "inner"), None),
        P(("group", "inner")),
        P(("group", "inner")),
        P("group", None, "inner"),
        P("group", None, "inner"),
        P("group", "inner", None),
    )
    out_specs = P(("group", "inner"), None)
    return jax.shard_map(body, mesh=mesh, in_specs=in_specs, out_specs=out_specs, check_vma=False)
```

```python
import functools

import jax
import jax.numpy as jnp
from jax import lax
from jax.experimental import pallas as pl
from jax.experimental.pallas import tpu as pltpu
from jax.sharding import PartitionSpec as P

MESH = pl.DeviceIdType.MESH


def torus_sides(groups):
    side = 4 if groups % 4 == 0 and groups > 4 else groups
    return groups // side, side


def chunk_orders(groups):
    if groups == 16:
        return [
            [(0, 0), (0, 2), (2, 0), (2, 2), (1, 2), (3, 2), (2, 1), (2, 3)],
            [(0, 1), (0, 3), (1, 0), (3, 0), (1, 1), (3, 3), (1, 3), (3, 1)],
        ]
    pairs = [((0, k), (0, groups - k)) for k in range(1, (groups + 1) // 2)]
    first = [(0, 0)] + ([(0, groups // 2)] if groups % 2 == 0 and groups > 1 else [])
    second = []
    for index, pair in enumerate(pairs):
        (first if index < len(pairs) // 2 else second).extend(pair)
    return [first, second] if second else [first]


def peer_of(me, offset, sign, groups):
    rows, side = torus_sides(groups)
    dz, dy = offset
    z = lax.rem(me // side + sign * dz + rows, rows)
    y = lax.rem(lax.rem(me, side) + sign * dy + side, side)
    return z * side + y


def exchange_kernel(groups, offsets, src_base, sign, x_ref, y_ref, local_sem, send_sem, recv_sem):
    me = lax.axis_index("group")
    inner = lax.axis_index("inner")
    peers = [k for k in offsets if k != (0, 0)]
    barrier = pltpu.get_barrier_semaphore()
    for k in peers:
        pl.semaphore_signal(
            barrier, inc=1, device_id=(peer_of(me, k, 1, groups), inner), device_id_type=MESH
        )
    if peers:
        pl.semaphore_wait(barrier, len(peers))
    local = None
    sends = []
    for i, k in enumerate(offsets):
        if k == (0, 0):
            local = pltpu.make_async_copy(x_ref.at[src_base + i], y_ref.at[i], local_sem)
            local.start()
            continue
        dest = peer_of(me, k, sign, groups)
        copy = pltpu.make_async_remote_copy(
            src_ref=x_ref.at[src_base + i],
            dst_ref=y_ref.at[i],
            send_sem=send_sem.at[i],
            recv_sem=recv_sem.at[i],
            device_id=(dest, inner),
            device_id_type=MESH,
        )
        copy.start()
        sends.append(copy)
    for copy in sends:
        copy.wait_send()
    for i, k in enumerate(offsets):
        if k == (0, 0):
            continue
        source = peer_of(me, k, -sign, groups)
        pltpu.make_async_remote_copy(
            src_ref=x_ref.at[src_base + i],
            dst_ref=y_ref.at[i],
            send_sem=send_sem.at[i],
            recv_sem=recv_sem.at[i],
            device_id=(source, inner),
            device_id_type=MESH,
        ).wait_recv()
    if local is not None:
        local.wait()


def group_exchange(x, offsets, src_base, sign, collective_id):
    groups = lax.axis_size("group")
    count = len(offsets)
    return pl.pallas_call(
        functools.partial(exchange_kernel, groups, tuple(offsets), src_base, sign),
        out_shape=jax.ShapeDtypeStruct((count,) + x.shape[1:], x.dtype),
        in_specs=[pl.BlockSpec(memory_space=pl.ANY)],
        out_specs=pl.BlockSpec(memory_space=pl.ANY),
        scratch_shapes=[
            pltpu.SemaphoreType.DMA,
            pltpu.SemaphoreType.DMA((count,)),
            pltpu.SemaphoreType.DMA((count,)),
        ],
        compiler_params=pltpu.CompilerParams(collective_id=collective_id, has_side_effects=True),
    )(x)


def swap_kernel(x_ref, y_ref, send_sem, recv_sem):
    group = lax.axis_index("group")
    inner = lax.axis_index("inner")
    core = lax.rem(inner, 2)
    partner = inner + 1 - 2 * core
    barrier = pltpu.get_barrier_semaphore()
    pl.semaphore_signal(barrier, inc=1, device_id=(group, partner), device_id_type=MESH)
    pl.semaphore_wait(barrier, 1)
    copy = pltpu.make_async_remote_copy(
        src_ref=x_ref.at[:, 1 - core],
        dst_ref=y_ref,
        send_sem=send_sem,
        recv_sem=recv_sem,
        device_id=(group, partner),
        device_id_type=MESH,
    )
    copy.start()
    copy.wait_send()
    copy.wait_recv()


def partner_swap(x, collective_id):
    return pl.pallas_call(
        swap_kernel,
        out_shape=jax.ShapeDtypeStruct(x.shape[:1] + x.shape[2:], x.dtype),
        in_specs=[pl.BlockSpec(memory_space=pl.ANY)],
        out_specs=pl.BlockSpec(memory_space=pl.ANY),
        scratch_shapes=[pltpu.SemaphoreType.DMA, pltpu.SemaphoreType.DMA],
        compiler_params=pltpu.CompilerParams(collective_id=collective_id, has_side_effects=True),
    )(x)


def expert_part(rows_in, gate_mat, up_mat, down_mat):
    gate_pre = jnp.dot(rows_in, gate_mat, preferred_element_type=jnp.float32)
    up_pre = jnp.dot(rows_in, up_mat, preferred_element_type=jnp.float32)
    hidden = (jax.nn.silu(gate_pre) * up_pre).astype(jnp.bfloat16)
    return jnp.dot(hidden, down_mat, preferred_element_type=jnp.float32)


def body(tokens, target, gate_scale, gate_weight, up_weight, down_weight):
    groups = lax.axis_size("group")
    tok_count = tokens.shape[0]
    model_width = tokens.shape[1]
    capacity = tok_count * 5 // (4 * groups)
    slot_count = groups * capacity
    chunks = chunk_orders(groups)
    order = [k for chunk in chunks for k in chunk]
    rows, side = torus_sides(groups)
    position_of = [0] * groups
    for position, (dz, dy) in enumerate(order):
        position_of[dz * side + dy] = position
    me = lax.axis_index("group")
    onehot = (target[:, None] == jnp.arange(groups, dtype=jnp.int32)[None, :]).astype(jnp.int32)
    rank_in = jnp.sum((jnp.cumsum(onehot, axis=0) - onehot) * onehot, axis=1)
    relative_z = lax.rem(target // side - me // side + rows, rows)
    relative_y = lax.rem(lax.rem(target, side) - lax.rem(me, side) + side, side)
    relative = jnp.where(target < groups, relative_z * side + relative_y, 0)
    position = jnp.asarray(position_of, dtype=jnp.int32)[relative]
    slot_of = jnp.where(target < groups, position * capacity + rank_in, slot_count)
    dispatch = (slot_of[None, :] == jnp.arange(slot_count, dtype=jnp.int32)[:, None]).astype(
        jnp.bfloat16
    )
    outbound = jnp.dot(dispatch, tokens, preferred_element_type=jnp.float32).astype(jnp.bfloat16)
    lanes = 128 if (capacity * model_width) % 128 == 0 else model_width
    slab = (capacity * model_width // lanes, lanes)
    returned = []
    base = 0
    for index, chunk in enumerate(chunks):
        piece = outbound[base * capacity : (base + len(chunk)) * capacity]
        received = group_exchange(piece.reshape((len(chunk),) + slab), chunk, 0, 1, 2 * index)
        base += len(chunk)
        rows = received.reshape(len(chunk) * capacity, model_width)
        gathered = lax.all_gather(rows, "inner", axis=0, tiled=True)
        partial_value = expert_part(gathered, gate_weight[0], up_weight[0], down_weight[0])
        inner_size = lax.axis_size("inner")
        if inner_size % 2 == 0:
            same_core = [list(range(c, inner_size, 2)) for c in range(2)]
            core = lax.rem(lax.axis_index("inner"), 2)
            by_core = partial_value.astype(jnp.bfloat16).reshape(inner_size // 2, 2, -1, model_width)
            received_sum = partner_swap(by_core, 8 + index)
            own_part = lax.dynamic_index_in_dim(by_core, core, axis=1, keepdims=False)
            pair_sum = own_part.astype(jnp.float32) + received_sum.astype(jnp.float32)
            summed = lax.psum_scatter(
                pair_sum.astype(jnp.bfloat16).reshape((-1,) + slab),
                "inner",
                scatter_dimension=0,
                tiled=True,
                axis_index_groups=same_core,
            )
        else:
            summed = lax.psum_scatter(
                partial_value.astype(jnp.bfloat16), "inner", scatter_dimension=0, tiled=True
            )
        returned.append((summed.reshape((len(chunk),) + slab), chunk, index))
    expert_out = None
    base = 0
    for z, chunk, index in returned:
        back_rows = group_exchange(z, chunk, 0, -1, 2 * index + 1)
        term = jnp.einsum(
            "gct,gcd->td",
            dispatch[base * capacity : (base + len(chunk)) * capacity].reshape(
                len(chunk), capacity, tok_count
            ),
            back_rows.reshape(len(chunk), capacity, model_width),
            preferred_element_type=jnp.float32,
        )
        base += len(chunk)
        expert_out = term if expert_out is None else expert_out + term
    return (gate_scale[:, None] * expert_out).astype(jnp.bfloat16)


def solution(mesh):
    in_specs = (
        P(("group", "inner"), None),
        P(("group", "inner")),
        P(("group", "inner")),
        P("group", None, "inner"),
        P("group", None, "inner"),
        P("group", "inner", None),
    )
    out_specs = P(("group", "inner"), None)
    return jax.shard_map(body, mesh=mesh, in_specs=in_specs, out_specs=out_specs, check_vma=False)
```

```python
import functools

import jax
import jax.numpy as jnp
from jax import lax
from jax.experimental import pallas as pl
from jax.experimental.pallas import tpu as pltpu
from jax.sharding import PartitionSpec as P

MESH = pl.DeviceIdType.MESH


def torus_sides(groups):
    side = 4 if groups % 4 == 0 and groups > 4 else groups
    return groups // side, side


def chunk_orders(groups):
    if groups == 16:
        return [
            [(0, 0), (0, 2), (2, 0), (2, 2), (1, 2), (3, 2), (2, 1), (2, 3)],
            [(0, 1), (0, 3), (1, 0), (3, 0), (1, 1), (3, 3), (1, 3), (3, 1)],
        ]
    pairs = [((0, k), (0, groups - k)) for k in range(1, (groups + 1) // 2)]
    first = [(0, 0)] + ([(0, groups // 2)] if groups % 2 == 0 and groups > 1 else [])
    second = []
    for index, pair in enumerate(pairs):
        (first if index < len(pairs) // 2 else second).extend(pair)
    return [first, second] if second else [first]


def peer_of(me, offset, sign, groups):
    rows, side = torus_sides(groups)
    dz, dy = offset
    z = lax.rem(me // side + sign * dz + rows, rows)
    y = lax.rem(lax.rem(me, side) + sign * dy + side, side)
    return z * side + y


def exchange_kernel(groups, offsets, src_base, sign, x_ref, y_ref, local_sem, send_sem, recv_sem):
    me = lax.axis_index("group")
    inner = lax.axis_index("inner")
    peers = [k for k in offsets if k != (0, 0)]
    barrier = pltpu.get_barrier_semaphore()
    for k in peers:
        pl.semaphore_signal(
            barrier, inc=1, device_id=(peer_of(me, k, 1, groups), inner), device_id_type=MESH
        )
    if peers:
        pl.semaphore_wait(barrier, len(peers))
    local = None
    sends = []
    for i, k in enumerate(offsets):
        if k == (0, 0):
            local = pltpu.make_async_copy(x_ref.at[src_base + i], y_ref.at[i], local_sem)
            local.start()
            continue
        dest = peer_of(me, k, sign, groups)
        copy = pltpu.make_async_remote_copy(
            src_ref=x_ref.at[src_base + i],
            dst_ref=y_ref.at[i],
            send_sem=send_sem.at[i],
            recv_sem=recv_sem.at[i],
            device_id=(dest, inner),
            device_id_type=MESH,
        )
        copy.start()
        sends.append(copy)
    for copy in sends:
        copy.wait_send()
    for i, k in enumerate(offsets):
        if k == (0, 0):
            continue
        source = peer_of(me, k, -sign, groups)
        pltpu.make_async_remote_copy(
            src_ref=x_ref.at[src_base + i],
            dst_ref=y_ref.at[i],
            send_sem=send_sem.at[i],
            recv_sem=recv_sem.at[i],
            device_id=(source, inner),
            device_id_type=MESH,
        ).wait_recv()
    if local is not None:
        local.wait()


def group_exchange(x, offsets, src_base, sign, collective_id):
    groups = lax.axis_size("group")
    count = len(offsets)
    return pl.pallas_call(
        functools.partial(exchange_kernel, groups, tuple(offsets), src_base, sign),
        out_shape=jax.ShapeDtypeStruct((count,) + x.shape[1:], x.dtype),
        in_specs=[pl.BlockSpec(memory_space=pl.ANY)],
        out_specs=pl.BlockSpec(memory_space=pl.ANY),
        scratch_shapes=[
            pltpu.SemaphoreType.DMA,
            pltpu.SemaphoreType.DMA((count,)),
            pltpu.SemaphoreType.DMA((count,)),
        ],
        compiler_params=pltpu.CompilerParams(collective_id=collective_id, has_side_effects=True),
    )(x)


def swap_kernel(x_ref, y_ref, send_sem, recv_sem):
    group = lax.axis_index("group")
    inner = lax.axis_index("inner")
    core = lax.rem(inner, 2)
    partner = inner + 1 - 2 * core
    barrier = pltpu.get_barrier_semaphore()
    pl.semaphore_signal(barrier, inc=1, device_id=(group, partner), device_id_type=MESH)
    pl.semaphore_wait(barrier, 1)
    copy = pltpu.make_async_remote_copy(
        src_ref=x_ref.at[:, 1 - core],
        dst_ref=y_ref,
        send_sem=send_sem,
        recv_sem=recv_sem,
        device_id=(group, partner),
        device_id_type=MESH,
    )
    copy.start()
    copy.wait_send()
    copy.wait_recv()


def partner_swap(x, collective_id):
    return pl.pallas_call(
        swap_kernel,
        out_shape=jax.ShapeDtypeStruct(x.shape[:1] + x.shape[2:], x.dtype),
        in_specs=[pl.BlockSpec(memory_space=pl.ANY)],
        out_specs=pl.BlockSpec(memory_space=pl.ANY),
        scratch_shapes=[pltpu.SemaphoreType.DMA, pltpu.SemaphoreType.DMA],
        compiler_params=pltpu.CompilerParams(collective_id=collective_id, has_side_effects=True),
    )(x)


def expert_part(rows_in, gate_mat, up_mat, down_mat):
    gate_pre = jnp.dot(rows_in, gate_mat, preferred_element_type=jnp.float32)
    up_pre = jnp.dot(rows_in, up_mat, preferred_element_type=jnp.float32)
    hidden = (jax.nn.silu(gate_pre) * up_pre).astype(jnp.bfloat16)
    return jnp.dot(hidden, down_mat, preferred_element_type=jnp.float32)


def body(tokens, target, gate_scale, gate_weight, up_weight, down_weight):
    groups = lax.axis_size("group")
    tok_count = tokens.shape[0]
    model_width = tokens.shape[1]
    capacity = tok_count * 5 // (4 * groups)
    slot_count = groups * capacity
    chunks = chunk_orders(groups)
    order = [k for chunk in chunks for k in chunk]
    rows, side = torus_sides(groups)
    position_of = [0] * groups
    for position, (dz, dy) in enumerate(order):
        position_of[dz * side + dy] = position
    me = lax.axis_index("group")
    onehot = (target[:, None] == jnp.arange(groups, dtype=jnp.int32)[None, :]).astype(jnp.int32)
    rank_in = jnp.sum((jnp.cumsum(onehot, axis=0) - onehot) * onehot, axis=1)
    relative_z = lax.rem(target // side - me // side + rows, rows)
    relative_y = lax.rem(lax.rem(target, side) - lax.rem(me, side) + side, side)
    relative = jnp.where(target < groups, relative_z * side + relative_y, 0)
    position = jnp.asarray(position_of, dtype=jnp.int32)[relative]
    slot_of = jnp.where(target < groups, position * capacity + rank_in, slot_count)
    dispatch = (slot_of[None, :] == jnp.arange(slot_count, dtype=jnp.int32)[:, None]).astype(
        jnp.bfloat16
    )
    outbound = jnp.dot(dispatch, tokens, preferred_element_type=jnp.float32).astype(jnp.bfloat16)
    lanes = 128 if (capacity * model_width) % 128 == 0 else model_width
    slab = (capacity * model_width // lanes, lanes)
    returned = []
    base = 0
    for index, chunk in enumerate(chunks):
        piece = outbound[base * capacity : (base + len(chunk)) * capacity]
        received = group_exchange(piece.reshape((len(chunk),) + slab), chunk, 0, 1, 2 * index)
        base += len(chunk)
        rows = received.reshape(len(chunk) * capacity, model_width)
        gathered = lax.all_gather(rows, "inner", axis=0, tiled=True)
        partial_value = expert_part(gathered, gate_weight[0], up_weight[0], down_weight[0])
        inner_size = lax.axis_size("inner")
        if inner_size % 2 == 0:
            same_core = [list(range(c, inner_size, 2)) for c in range(2)]
            core = lax.rem(lax.axis_index("inner"), 2)
            by_core = partial_value.astype(jnp.bfloat16).reshape(inner_size // 2, 2, -1, model_width)
            received_sum = partner_swap(by_core, 8 + index)
            own_part = lax.dynamic_index_in_dim(by_core, core, axis=1, keepdims=False)
            pair_sum = own_part.astype(jnp.float32) + received_sum.astype(jnp.float32)
            summed = lax.psum_scatter(
                pair_sum.astype(jnp.bfloat16).reshape((-1,) + slab),
                "inner",
                scatter_dimension=0,
                tiled=True,
                axis_index_groups=same_core,
            )
        else:
            summed = lax.psum_scatter(
                partial_value.astype(jnp.bfloat16), "inner", scatter_dimension=0, tiled=True
            )
        returned.append((summed.reshape((len(chunk),) + slab), chunk, index))
    expert_out = None
    base = 0
    for z, chunk, index in returned:
        if expert_out is not None:
            z, expert_out = lax.optimization_barrier((z, expert_out))
        back_rows = group_exchange(z, chunk, 0, -1, 2 * index + 1)
        term = jnp.einsum(
            "gct,gcd->td",
            dispatch[base * capacity : (base + len(chunk)) * capacity].reshape(
                len(chunk), capacity, tok_count
            ),
            back_rows.reshape(len(chunk), capacity, model_width),
            preferred_element_type=jnp.float32,
        )
        base += len(chunk)
        expert_out = term if expert_out is None else expert_out + term
    return (gate_scale[:, None] * expert_out).astype(jnp.bfloat16)


def solution(mesh):
    in_specs = (
        P(("group", "inner"), None),
        P(("group", "inner")),
        P(("group", "inner")),
        P("group", None, "inner"),
        P("group", None, "inner"),
        P("group", "inner", None),
    )
    out_specs = P(("group", "inner"), None)
    return jax.shard_map(body, mesh=mesh, in_specs=in_specs, out_specs=out_specs, check_vma=False)
```

```python
import functools

import jax
import jax.numpy as jnp
from jax import lax
from jax.experimental import pallas as pl
from jax.experimental.pallas import tpu as pltpu
from jax.sharding import PartitionSpec as P

MESH = pl.DeviceIdType.MESH


def torus_sides(groups):
    side = 4 if groups % 4 == 0 and groups > 4 else groups
    return groups // side, side


def chunk_orders(groups):
    if groups == 16:
        return [
            [(0, 0), (0, 2), (2, 0), (2, 2), (1, 2), (3, 2), (2, 1), (2, 3)],
            [(0, 1), (0, 3), (1, 0), (3, 0), (1, 1), (3, 3), (1, 3), (3, 1)],
        ]
    pairs = [((0, k), (0, groups - k)) for k in range(1, (groups + 1) // 2)]
    first = [(0, 0)] + ([(0, groups // 2)] if groups % 2 == 0 and groups > 1 else [])
    second = []
    for index, pair in enumerate(pairs):
        (first if index < len(pairs) // 2 else second).extend(pair)
    return [first, second] if second else [first]


def peer_of(me, offset, sign, groups):
    rows, side = torus_sides(groups)
    dz, dy = offset
    z = lax.rem(me // side + sign * dz + rows, rows)
    y = lax.rem(lax.rem(me, side) + sign * dy + side, side)
    return z * side + y


def exchange_kernel(groups, offsets, src_base, sign, x_ref, y_ref, local_sem, send_sem, recv_sem):
    me = lax.axis_index("group")
    inner = lax.axis_index("inner")
    peers = [k for k in offsets if k != (0, 0)]
    barrier = pltpu.get_barrier_semaphore()
    for k in peers:
        pl.semaphore_signal(
            barrier, inc=1, device_id=(peer_of(me, k, 1, groups), inner), device_id_type=MESH
        )
    if peers:
        pl.semaphore_wait(barrier, len(peers))
    sends = []
    for i, k in enumerate(offsets):
        if k == (0, 0):
            continue
        dest = peer_of(me, k, sign, groups)
        copy = pltpu.make_async_remote_copy(
            src_ref=x_ref.at[src_base + i],
            dst_ref=y_ref.at[i],
            send_sem=send_sem.at[i],
            recv_sem=recv_sem.at[i],
            device_id=(dest, inner),
            device_id_type=MESH,
        )
        copy.start()
        sends.append(copy)
    for copy in sends:
        copy.wait_send()
    for i, k in enumerate(offsets):
        if k == (0, 0):
            continue
        source = peer_of(me, k, -sign, groups)
        pltpu.make_async_remote_copy(
            src_ref=x_ref.at[src_base + i],
            dst_ref=y_ref.at[i],
            send_sem=send_sem.at[i],
            recv_sem=recv_sem.at[i],
            device_id=(source, inner),
            device_id_type=MESH,
        ).wait_recv()


def group_exchange(x, offsets, src_base, sign, collective_id):
    groups = lax.axis_size("group")
    count = len(offsets)
    out = pl.pallas_call(
        functools.partial(exchange_kernel, groups, tuple(offsets), src_base, sign),
        out_shape=jax.ShapeDtypeStruct((count,) + x.shape[1:], x.dtype),
        in_specs=[pl.BlockSpec(memory_space=pl.ANY)],
        out_specs=pl.BlockSpec(memory_space=pl.ANY),
        scratch_shapes=[
            pltpu.SemaphoreType.DMA,
            pltpu.SemaphoreType.DMA((count,)),
            pltpu.SemaphoreType.DMA((count,)),
        ],
        compiler_params=pltpu.CompilerParams(collective_id=collective_id, has_side_effects=True),
    )(x)
    for i, k in enumerate(offsets):
        if k == (0, 0):
            out = out.at[i].set(x[src_base + i])
    return out


def swap_kernel(x_ref, y_ref, send_sem, recv_sem):
    group = lax.axis_index("group")
    inner = lax.axis_index("inner")
    core = lax.rem(inner, 2)
    partner = inner + 1 - 2 * core
    barrier = pltpu.get_barrier_semaphore()
    pl.semaphore_signal(barrier, inc=1, device_id=(group, partner), device_id_type=MESH)
    pl.semaphore_wait(barrier, 1)
    copy = pltpu.make_async_remote_copy(
        src_ref=x_ref.at[:, 1 - core],
        dst_ref=y_ref,
        send_sem=send_sem,
        recv_sem=recv_sem,
        device_id=(group, partner),
        device_id_type=MESH,
    )
    copy.start()
    copy.wait_send()
    copy.wait_recv()


def partner_swap(x, collective_id):
    return pl.pallas_call(
        swap_kernel,
        out_shape=jax.ShapeDtypeStruct(x.shape[:1] + x.shape[2:], x.dtype),
        in_specs=[pl.BlockSpec(memory_space=pl.ANY)],
        out_specs=pl.BlockSpec(memory_space=pl.ANY),
        scratch_shapes=[pltpu.SemaphoreType.DMA, pltpu.SemaphoreType.DMA],
        compiler_params=pltpu.CompilerParams(collective_id=collective_id, has_side_effects=True),
    )(x)


def expert_part(rows_in, gate_mat, up_mat, down_mat):
    gate_pre = jnp.dot(rows_in, gate_mat, preferred_element_type=jnp.float32)
    up_pre = jnp.dot(rows_in, up_mat, preferred_element_type=jnp.float32)
    hidden = (jax.nn.silu(gate_pre) * up_pre).astype(jnp.bfloat16)
    return jnp.dot(hidden, down_mat, preferred_element_type=jnp.float32)


def body(tokens, target, gate_scale, gate_weight, up_weight, down_weight):
    groups = lax.axis_size("group")
    tok_count = tokens.shape[0]
    model_width = tokens.shape[1]
    capacity = tok_count * 5 // (4 * groups)
    slot_count = groups * capacity
    chunks = chunk_orders(groups)
    order = [k for chunk in chunks for k in chunk]
    rows, side = torus_sides(groups)
    position_of = [0] * groups
    for position, (dz, dy) in enumerate(order):
        position_of[dz * side + dy] = position
    me = lax.axis_index("group")
    onehot = (target[:, None] == jnp.arange(groups, dtype=jnp.int32)[None, :]).astype(jnp.int32)
    rank_in = jnp.sum((jnp.cumsum(onehot, axis=0) - onehot) * onehot, axis=1)
    relative_z = lax.rem(target // side - me // side + rows, rows)
    relative_y = lax.rem(lax.rem(target, side) - lax.rem(me, side) + side, side)
    relative = jnp.where(target < groups, relative_z * side + relative_y, 0)
    position = jnp.asarray(position_of, dtype=jnp.int32)[relative]
    slot_of = jnp.where(target < groups, position * capacity + rank_in, slot_count)
    dispatch = (slot_of[None, :] == jnp.arange(slot_count, dtype=jnp.int32)[:, None]).astype(
        jnp.bfloat16
    )
    outbound = jnp.dot(dispatch, tokens, preferred_element_type=jnp.float32).astype(jnp.bfloat16)
    lanes = 128 if (capacity * model_width) % 128 == 0 else model_width
    slab = (capacity * model_width // lanes, lanes)
    returned = []
    base = 0
    for index, chunk in enumerate(chunks):
        piece = outbound[base * capacity : (base + len(chunk)) * capacity]
        received = group_exchange(piece.reshape((len(chunk),) + slab), chunk, 0, 1, 2 * index)
        base += len(chunk)
        rows = received.reshape(len(chunk) * capacity, model_width)
        gathered = lax.all_gather(rows, "inner", axis=0, tiled=True)
        partial_value = expert_part(gathered, gate_weight[0], up_weight[0], down_weight[0])
        inner_size = lax.axis_size("inner")
        if inner_size % 2 == 0:
            same_core = [list(range(c, inner_size, 2)) for c in range(2)]
            core = lax.rem(lax.axis_index("inner"), 2)
            by_core = partial_value.astype(jnp.bfloat16).reshape(inner_size // 2, 2, -1, model_width)
            received_sum = partner_swap(by_core, 8 + index)
            own_part = lax.dynamic_index_in_dim(by_core, core, axis=1, keepdims=False)
            pair_sum = own_part.astype(jnp.float32) + received_sum.astype(jnp.float32)
            summed = lax.psum_scatter(
                pair_sum.astype(jnp.bfloat16).reshape((-1,) + slab),
                "inner",
                scatter_dimension=0,
                tiled=True,
                axis_index_groups=same_core,
            )
        else:
            summed = lax.psum_scatter(
                partial_value.astype(jnp.bfloat16), "inner", scatter_dimension=0, tiled=True
            )
        returned.append((summed.reshape((len(chunk),) + slab), chunk, index))
    expert_out = None
    base = 0
    for z, chunk, index in returned:
        back_rows = group_exchange(z, chunk, 0, -1, 2 * index + 1)
        term = jnp.einsum(
            "gct,gcd->td",
            dispatch[base * capacity : (base + len(chunk)) * capacity].reshape(
                len(chunk), capacity, tok_count
            ),
            back_rows.reshape(len(chunk), capacity, model_width),
            preferred_element_type=jnp.float32,
        )
        base += len(chunk)
        expert_out = term if expert_out is None else expert_out + term
    return (gate_scale[:, None] * expert_out).astype(jnp.bfloat16)


def solution(mesh):
    in_specs = (
        P(("group", "inner"), None),
        P(("group", "inner")),
        P(("group", "inner")),
        P("group", None, "inner"),
        P("group", None, "inner"),
        P("group", "inner", None),
    )
    out_specs = P(("group", "inner"), None)
    return jax.shard_map(body, mesh=mesh, in_specs=in_specs, out_specs=out_specs, check_vma=False)
```

```python
import functools

import jax
import jax.numpy as jnp
from jax import lax
from jax.experimental import pallas as pl
from jax.experimental.pallas import tpu as pltpu
from jax.sharding import PartitionSpec as P

MESH = pl.DeviceIdType.MESH


def torus_sides(groups):
    side = 4 if groups % 4 == 0 and groups > 4 else groups
    return groups // side, side


def chunk_orders(groups):
    if groups == 16:
        return [
            [(0, 0), (0, 2), (2, 0), (2, 2), (1, 2), (3, 2), (2, 1), (2, 3)],
            [(0, 1), (0, 3), (1, 0), (3, 0), (1, 1), (3, 3), (1, 3), (3, 1)],
        ]
    pairs = [((0, k), (0, groups - k)) for k in range(1, (groups + 1) // 2)]
    first = [(0, 0)] + ([(0, groups // 2)] if groups % 2 == 0 and groups > 1 else [])
    second = []
    for index, pair in enumerate(pairs):
        (first if index < len(pairs) // 2 else second).extend(pair)
    return [first, second] if second else [first]


def peer_of(me, offset, sign, groups):
    rows, side = torus_sides(groups)
    dz, dy = offset
    z = lax.rem(me // side + sign * dz + rows, rows)
    y = lax.rem(lax.rem(me, side) + sign * dy + side, side)
    return z * side + y


def exchange_kernel(groups, offsets, src_base, sign, x_ref, y_ref, local_sem, send_sem, recv_sem):
    me = lax.axis_index("group")
    inner = lax.axis_index("inner")
    peers = [k for k in offsets if k != (0, 0)]
    barrier = pltpu.get_barrier_semaphore()
    for k in peers:
        pl.semaphore_signal(
            barrier, inc=1, device_id=(peer_of(me, k, 1, groups), inner), device_id_type=MESH
        )
    if peers:
        pl.semaphore_wait(barrier, len(peers))
    local = None
    sends = []
    for i, k in enumerate(offsets):
        if k == (0, 0):
            local = pltpu.make_async_copy(x_ref.at[src_base + i], y_ref.at[i], local_sem)
            local.start()
            continue
        dest = peer_of(me, k, sign, groups)
        copy = pltpu.make_async_remote_copy(
            src_ref=x_ref.at[src_base + i],
            dst_ref=y_ref.at[i],
            send_sem=send_sem.at[i],
            recv_sem=recv_sem.at[i],
            device_id=(dest, inner),
            device_id_type=MESH,
        )
        copy.start()
        sends.append(copy)
    for copy in sends:
        copy.wait_send()
    for i, k in enumerate(offsets):
        if k == (0, 0):
            continue
        source = peer_of(me, k, -sign, groups)
        pltpu.make_async_remote_copy(
            src_ref=x_ref.at[src_base + i],
            dst_ref=y_ref.at[i],
            send_sem=send_sem.at[i],
            recv_sem=recv_sem.at[i],
            device_id=(source, inner),
            device_id_type=MESH,
        ).wait_recv()
    if local is not None:
        local.wait()


def group_exchange(x, offsets, src_base, sign, collective_id):
    groups = lax.axis_size("group")
    count = len(offsets)
    return pl.pallas_call(
        functools.partial(exchange_kernel, groups, tuple(offsets), src_base, sign),
        out_shape=jax.ShapeDtypeStruct((count,) + x.shape[1:], x.dtype),
        in_specs=[pl.BlockSpec(memory_space=pl.ANY)],
        out_specs=pl.BlockSpec(memory_space=pl.ANY),
        scratch_shapes=[
            pltpu.SemaphoreType.DMA,
            pltpu.SemaphoreType.DMA((count,)),
            pltpu.SemaphoreType.DMA((count,)),
        ],
        compiler_params=pltpu.CompilerParams(collective_id=collective_id, has_side_effects=True),
    )(x)


def swap_kernel(x_ref, y_ref, send_sem, recv_sem):
    group = lax.axis_index("group")
    inner = lax.axis_index("inner")
    core = lax.rem(inner, 2)
    partner = inner + 1 - 2 * core
    barrier = pltpu.get_barrier_semaphore()
    pl.semaphore_signal(barrier, inc=1, device_id=(group, partner), device_id_type=MESH)
    pl.semaphore_wait(barrier, 1)
    copy = pltpu.make_async_remote_copy(
        src_ref=x_ref.at[:, 1 - core],
        dst_ref=y_ref,
        send_sem=send_sem,
        recv_sem=recv_sem,
        device_id=(group, partner),
        device_id_type=MESH,
    )
    copy.start()
    copy.wait_send()
    copy.wait_recv()


def partner_swap(x, collective_id):
    return pl.pallas_call(
        swap_kernel,
        out_shape=jax.ShapeDtypeStruct(x.shape[:1] + x.shape[2:], x.dtype),
        in_specs=[pl.BlockSpec(memory_space=pl.ANY)],
        out_specs=pl.BlockSpec(memory_space=pl.ANY),
        scratch_shapes=[pltpu.SemaphoreType.DMA, pltpu.SemaphoreType.DMA],
        compiler_params=pltpu.CompilerParams(collective_id=collective_id, has_side_effects=True),
    )(x)


def expert_part(rows_in, gate_mat, up_mat, down_mat):
    gate_pre = jnp.dot(rows_in, gate_mat, preferred_element_type=jnp.float32)
    up_pre = jnp.dot(rows_in, up_mat, preferred_element_type=jnp.float32)
    hidden = (jax.nn.silu(gate_pre) * up_pre).astype(jnp.bfloat16)
    return jnp.dot(hidden, down_mat, preferred_element_type=jnp.float32)


def body(tokens, target, gate_scale, gate_weight, up_weight, down_weight):
    groups = lax.axis_size("group")
    tok_count = tokens.shape[0]
    model_width = tokens.shape[1]
    capacity = tok_count * 5 // (4 * groups)
    slot_count = groups * capacity
    chunks = chunk_orders(groups)
    order = [k for chunk in chunks for k in chunk]
    rows, side = torus_sides(groups)
    position_of = [0] * groups
    for position, (dz, dy) in enumerate(order):
        position_of[dz * side + dy] = position
    me = lax.axis_index("group")
    onehot = (target[:, None] == jnp.arange(groups, dtype=jnp.int32)[None, :]).astype(jnp.int32)
    earlier = (
        jnp.arange(tok_count, dtype=jnp.int32)[:, None] > jnp.arange(tok_count, dtype=jnp.int32)[None, :]
    ).astype(jnp.bfloat16)
    before = jnp.dot(earlier, onehot.astype(jnp.bfloat16), preferred_element_type=jnp.float32)
    rank_in = jnp.sum(before * onehot, axis=1).astype(jnp.int32)
    relative_z = lax.rem(target // side - me // side + rows, rows)
    relative_y = lax.rem(lax.rem(target, side) - lax.rem(me, side) + side, side)
    relative = jnp.where(target < groups, relative_z * side + relative_y, 0)
    position = jnp.asarray(position_of, dtype=jnp.int32)[relative]
    slot_of = jnp.where(target < groups, position * capacity + rank_in, slot_count)
    dispatch = (slot_of[None, :] == jnp.arange(slot_count, dtype=jnp.int32)[:, None]).astype(
        jnp.bfloat16
    )
    outbound = jnp.dot(dispatch, tokens, preferred_element_type=jnp.float32).astype(jnp.bfloat16)
    lanes = 128 if (capacity * model_width) % 128 == 0 else model_width
    slab = (capacity * model_width // lanes, lanes)
    returned = []
    base = 0
    for index, chunk in enumerate(chunks):
        piece = outbound[base * capacity : (base + len(chunk)) * capacity]
        received = group_exchange(piece.reshape((len(chunk),) + slab), chunk, 0, 1, 2 * index)
        base += len(chunk)
        rows = received.reshape(len(chunk) * capacity, model_width)
        gathered = lax.all_gather(rows, "inner", axis=0, tiled=True)
        partial_value = expert_part(gathered, gate_weight[0], up_weight[0], down_weight[0])
        inner_size = lax.axis_size("inner")
        if inner_size % 2 == 0:
            same_core = [list(range(c, inner_size, 2)) for c in range(2)]
            core = lax.rem(lax.axis_index("inner"), 2)
            by_core = partial_value.astype(jnp.bfloat16).reshape(inner_size // 2, 2, -1, model_width)
            received_sum = partner_swap(by_core, 8 + index)
            own_part = lax.dynamic_index_in_dim(by_core, core, axis=1, keepdims=False)
            pair_sum = own_part.astype(jnp.float32) + received_sum.astype(jnp.float32)
            summed = lax.psum_scatter(
                pair_sum.astype(jnp.bfloat16).reshape((-1,) + slab),
                "inner",
                scatter_dimension=0,
                tiled=True,
                axis_index_groups=same_core,
            )
        else:
            summed = lax.psum_scatter(
                partial_value.astype(jnp.bfloat16), "inner", scatter_dimension=0, tiled=True
            )
        returned.append((summed.reshape((len(chunk),) + slab), chunk, index))
    expert_out = None
    base = 0
    for z, chunk, index in returned:
        back_rows = group_exchange(z, chunk, 0, -1, 2 * index + 1)
        term = jnp.einsum(
            "gct,gcd->td",
            dispatch[base * capacity : (base + len(chunk)) * capacity].reshape(
                len(chunk), capacity, tok_count
            ),
            back_rows.reshape(len(chunk), capacity, model_width),
            preferred_element_type=jnp.float32,
        )
        base += len(chunk)
        expert_out = term if expert_out is None else expert_out + term
    return (gate_scale[:, None] * expert_out).astype(jnp.bfloat16)


def solution(mesh):
    in_specs = (
        P(("group", "inner"), None),
        P(("group", "inner")),
        P(("group", "inner")),
        P("group", None, "inner"),
        P("group", None, "inner"),
        P("group", "inner", None),
    )
    out_specs = P(("group", "inner"), None)
    return jax.shard_map(body, mesh=mesh, in_specs=in_specs, out_specs=out_specs, check_vma=False)
```

```python
import functools

import jax
import jax.numpy as jnp
from jax import lax
from jax.experimental import pallas as pl
from jax.experimental.pallas import tpu as pltpu
from jax.sharding import PartitionSpec as P

MESH = pl.DeviceIdType.MESH


def torus_sides(groups):
    side = 4 if groups % 4 == 0 and groups > 4 else groups
    return groups // side, side


def chunk_orders(groups):
    if groups == 16:
        return [
            [(0, 0), (0, 2), (2, 0), (2, 2), (1, 2), (3, 2), (2, 1), (2, 3)],
            [(0, 1), (0, 3), (1, 0), (3, 0), (1, 1), (3, 3), (1, 3), (3, 1)],
        ]
    pairs = [((0, k), (0, groups - k)) for k in range(1, (groups + 1) // 2)]
    first = [(0, 0)] + ([(0, groups // 2)] if groups % 2 == 0 and groups > 1 else [])
    second = []
    for index, pair in enumerate(pairs):
        (first if index < len(pairs) // 2 else second).extend(pair)
    return [first, second] if second else [first]


def peer_of(me, offset, sign, groups):
    rows, side = torus_sides(groups)
    dz, dy = offset
    z = lax.rem(me // side + sign * dz + rows, rows)
    y = lax.rem(lax.rem(me, side) + sign * dy + side, side)
    return z * side + y


def exchange_kernel(groups, offsets, src_base, sign, x_ref, y_ref, local_sem, send_sem, recv_sem):
    me = lax.axis_index("group")
    inner = lax.axis_index("inner")
    peers = [k for k in offsets if k != (0, 0)]
    barrier = pltpu.get_barrier_semaphore()
    for k in peers:
        pl.semaphore_signal(
            barrier, inc=1, device_id=(peer_of(me, k, 1, groups), inner), device_id_type=MESH
        )
    if peers:
        pl.semaphore_wait(barrier, len(peers))
    local = None
    sends = []
    for i, k in enumerate(offsets):
        if k == (0, 0):
            local = pltpu.make_async_copy(x_ref.at[src_base + i], y_ref.at[i], local_sem)
            local.start()
            continue
        dest = peer_of(me, k, sign, groups)
        copy = pltpu.make_async_remote_copy(
            src_ref=x_ref.at[src_base + i],
            dst_ref=y_ref.at[i],
            send_sem=send_sem.at[i],
            recv_sem=recv_sem.at[i],
            device_id=(dest, inner),
            device_id_type=MESH,
        )
        copy.start()
        sends.append(copy)
    for copy in sends:
        copy.wait_send()
    for i, k in enumerate(offsets):
        if k == (0, 0):
            continue
        source = peer_of(me, k, -sign, groups)
        pltpu.make_async_remote_copy(
            src_ref=x_ref.at[src_base + i],
            dst_ref=y_ref.at[i],
            send_sem=send_sem.at[i],
            recv_sem=recv_sem.at[i],
            device_id=(source, inner),
            device_id_type=MESH,
        ).wait_recv()
    if local is not None:
        local.wait()


def group_exchange(x, offsets, src_base, sign, collective_id):
    groups = lax.axis_size("group")
    count = len(offsets)
    return pl.pallas_call(
        functools.partial(exchange_kernel, groups, tuple(offsets), src_base, sign),
        out_shape=jax.ShapeDtypeStruct((count,) + x.shape[1:], x.dtype),
        in_specs=[pl.BlockSpec(memory_space=pl.ANY)],
        out_specs=pl.BlockSpec(memory_space=pl.ANY),
        scratch_shapes=[
            pltpu.SemaphoreType.DMA,
            pltpu.SemaphoreType.DMA((count,)),
            pltpu.SemaphoreType.DMA((count,)),
        ],
        compiler_params=pltpu.CompilerParams(collective_id=collective_id, has_side_effects=True),
    )(x)


def swap_kernel(x_ref, y_ref, send_sem, recv_sem):
    group = lax.axis_index("group")
    inner = lax.axis_index("inner")
    core = lax.rem(inner, 2)
    partner = inner + 1 - 2 * core
    barrier = pltpu.get_barrier_semaphore()
    pl.semaphore_signal(barrier, inc=1, device_id=(group, partner), device_id_type=MESH)
    pl.semaphore_wait(barrier, 1)
    copy = pltpu.make_async_remote_copy(
        src_ref=x_ref.at[:, 1 - core],
        dst_ref=y_ref,
        send_sem=send_sem,
        recv_sem=recv_sem,
        device_id=(group, partner),
        device_id_type=MESH,
    )
    copy.start()
    copy.wait_send()
    copy.wait_recv()


def partner_swap(x, collective_id):
    return pl.pallas_call(
        swap_kernel,
        out_shape=jax.ShapeDtypeStruct(x.shape[:1] + x.shape[2:], x.dtype),
        in_specs=[pl.BlockSpec(memory_space=pl.ANY)],
        out_specs=pl.BlockSpec(memory_space=pl.ANY),
        scratch_shapes=[pltpu.SemaphoreType.DMA, pltpu.SemaphoreType.DMA],
        compiler_params=pltpu.CompilerParams(collective_id=collective_id, has_side_effects=True),
    )(x)


def expert_part(rows_in, gate_mat, up_mat, down_mat):
    gate_pre = jnp.dot(rows_in, gate_mat, preferred_element_type=jnp.float32)
    up_pre = jnp.dot(rows_in, up_mat, preferred_element_type=jnp.float32)
    hidden = (jax.nn.silu(gate_pre) * up_pre).astype(jnp.bfloat16)
    return jnp.dot(hidden, down_mat, preferred_element_type=jnp.float32)


def body(tokens, target, gate_scale, gate_weight, up_weight, down_weight):
    groups = lax.axis_size("group")
    tok_count = tokens.shape[0]
    model_width = tokens.shape[1]
    capacity = tok_count * 5 // (4 * groups)
    slot_count = groups * capacity
    chunks = chunk_orders(groups)
    order = [k for chunk in chunks for k in chunk]
    rows, side = torus_sides(groups)
    position_of = [0] * groups
    for position, (dz, dy) in enumerate(order):
        position_of[dz * side + dy] = position
    me = lax.axis_index("group")
    onehot = (target[:, None] == jnp.arange(groups, dtype=jnp.int32)[None, :]).astype(jnp.int32)
    earlier = (
        jnp.arange(tok_count, dtype=jnp.int32)[:, None] > jnp.arange(tok_count, dtype=jnp.int32)[None, :]
    ).astype(jnp.bfloat16)
    before = jnp.dot(earlier, onehot.astype(jnp.bfloat16), preferred_element_type=jnp.float32)
    rank_in = jnp.sum(before * onehot, axis=1).astype(jnp.int32)
    relative_z = lax.rem(target // side - me // side + rows, rows)
    relative_y = lax.rem(lax.rem(target, side) - lax.rem(me, side) + side, side)
    relative = jnp.where(target < groups, relative_z * side + relative_y, 0)
    position = jnp.asarray(position_of, dtype=jnp.int32)[relative]
    slot_of = jnp.where(target < groups, position * capacity + rank_in, slot_count)
    dispatch = (slot_of[None, :] == jnp.arange(slot_count, dtype=jnp.int32)[:, None]).astype(
        jnp.bfloat16
    )
    lanes = 128 if (capacity * model_width) % 128 == 0 else model_width
    slab = (capacity * model_width // lanes, lanes)
    returned = []
    base = 0
    for index, chunk in enumerate(chunks):
        piece = jnp.dot(
            dispatch[base * capacity : (base + len(chunk)) * capacity],
            tokens,
            preferred_element_type=jnp.float32,
        ).astype(jnp.bfloat16)
        received = group_exchange(piece.reshape((len(chunk),) + slab), chunk, 0, 1, 2 * index)
        base += len(chunk)
        rows = received.reshape(len(chunk) * capacity, model_width)
        gathered = lax.all_gather(rows, "inner", axis=0, tiled=True)
        partial_value = expert_part(gathered, gate_weight[0], up_weight[0], down_weight[0])
        inner_size = lax.axis_size("inner")
        if inner_size % 2 == 0:
            same_core = [list(range(c, inner_size, 2)) for c in range(2)]
            core = lax.rem(lax.axis_index("inner"), 2)
            by_core = partial_value.astype(jnp.bfloat16).reshape(inner_size // 2, 2, -1, model_width)
            received_sum = partner_swap(by_core, 8 + index)
            own_part = lax.dynamic_index_in_dim(by_core, core, axis=1, keepdims=False)
            pair_sum = own_part.astype(jnp.float32) + received_sum.astype(jnp.float32)
            summed = lax.psum_scatter(
                pair_sum.astype(jnp.bfloat16).reshape((-1,) + slab),
                "inner",
                scatter_dimension=0,
                tiled=True,
                axis_index_groups=same_core,
            )
        else:
            summed = lax.psum_scatter(
                partial_value.astype(jnp.bfloat16), "inner", scatter_dimension=0, tiled=True
            )
        returned.append((summed.reshape((len(chunk),) + slab), chunk, index))
    expert_out = None
    base = 0
    for z, chunk, index in returned:
        back_rows = group_exchange(z, chunk, 0, -1, 2 * index + 1)
        term = jnp.einsum(
            "gct,gcd->td",
            dispatch[base * capacity : (base + len(chunk)) * capacity].reshape(
                len(chunk), capacity, tok_count
            ),
            back_rows.reshape(len(chunk), capacity, model_width),
            preferred_element_type=jnp.float32,
        )
        base += len(chunk)
        expert_out = term if expert_out is None else expert_out + term
    return (gate_scale[:, None] * expert_out).astype(jnp.bfloat16)


def solution(mesh):
    in_specs = (
        P(("group", "inner"), None),
        P(("group", "inner")),
        P(("group", "inner")),
        P("group", None, "inner"),
        P("group", None, "inner"),
        P("group", "inner", None),
    )
    out_specs = P(("group", "inner"), None)
    return jax.shard_map(body, mesh=mesh, in_specs=in_specs, out_specs=out_specs, check_vma=False)
```
